512 devices in a mesh: dp: 16 (over z_lo, y), ctx: 32 (over z_hi, x, core).
Axes of the slice: x: 4, y: 4, z: 16 (z_hi: 4, z_lo: 4; z = z_hi * 4 + z_lo), core: 2. Of those that a mesh axis runs over, the one named last changes fastest.
Arguments:
- tokens_in: bfloat16 [16, 6144, 2880], P('dp', 'ctx'), may hold values from -6 to 6
- queries: bfloat16 [16, 6144, 2048], P('dp', 'ctx'), may hold values from -20 to 20
- values_in: bfloat16 [16, 6144, 256], P('dp', 'ctx'), may hold values from -6 to 6
- key_weight: bfloat16 [2880, 256], P('dp', 'ctx'), may hold values from -0.109375 to 0.109375
- out_grad: bfloat16 [16, 6144, 2048], P('dp', 'ctx'), may hold values from -6 to 6
- doc_ids: int32 [16, 6144], P('dp'), may hold values from 0 to 15, never falling along the last dimension, each value on 1 to 768 neighbouring positions
Outputs:
- query_grad: bfloat16 [16, 6144, 2048], P('dp', 'ctx')
- value_grad: bfloat16 [16, 6144, 256], P('dp', 'ctx')
- input_grad: bfloat16 [16, 6144, 2880], P('dp', 'ctx')
- key_weight_grad: float32 [2880, 256], P('dp', 'ctx')
The draws below stay inside these ranges and needn't reach their ends.
Inputs may be any that keep to these rules, and one draw needn't show every extreme that they name: `doc_ids`: ids never fall along a sequence; a document has at most 768 tokens.
All inputs are finite; a program needn't handle non-finite values.
Results may differ from the reference program's by a relative error of at most 0.02.
The reference program's roundings to bfloat16 on the way count: a program that leaves them out, or rounds other values in their place, can miss the bound.
Values may be sent and summed in bfloat16 or wider, within the bound.
No kernel may reach another device: no remote copies, remote signals or barrier semaphores. Data moves between devices by JAX's collectives and lax.ppermute only.
A program may use at most 64 MiB of HBM per device.

```python
import math
import jax
import jax.numpy as jnp
import numpy as np
from jax import lax

D = 2880
QUERY_HEAD_COUNT = 32
KEY_VALUE_HEADS = 4
HEAD_SIZE = 64
WINDOW_LENGTH = 128
QW = 2048
KEY_FEATURES = 256
BATCH = 16
SEQUENCE_LENGTH = 6144
DOCS = 16
DOC_MOST = 768


def draw_queries(key, part):
    base_key = jax.random.fold_in(jax.random.fold_in(key, 17), 0)
    shape = (BATCH, SEQUENCE_LENGTH, QUERY_HEAD_COUNT * HEAD_SIZE)
    result = jnp.clip(jax.random.normal(base_key, shape, jnp.float32), -6.0, 6.0)
    return result.astype(jnp.bfloat16)


def levels(rng, shape, cuts, smallest, largest):
    def one(dim, parts):
        heights = jax.random.uniform(jax.random.fold_in(jax.random.fold_in(rng, 6), dim), (parts,), jnp.float32, smallest / len(cuts), largest / len(cuts))
        return jnp.repeat(jnp.exp(heights), shape[dim] // parts).reshape((-1,) + (1,) * (len(shape) - dim - 1))

    level = one(*cuts[0])
    for cut in cuts[1:]:
        level = level * one(*cut)
    return level


def split_up(amount, total, limit, skew):
    weights = [(1 << 20) // math.isqrt(rank ** skew) + 1 for rank in range(2, amount + 1)]
    spare, counts = total - limit - (amount - 1), [1] * (amount - 1)
    while spare > 0:
        movable = [i for i in range(amount - 1) if counts[i] < limit]
        pool, remaining = sum([weights[i] for i in movable]), spare
        for i in movable:
            extra = min(limit - counts[i], max(1, remaining * weights[i] // pool), spare)
            counts[i] = counts[i] + extra
            spare = spare - extra
    return np.array([limit] + counts)


def ragged(rng, amount, total, bound, lean):
    if amount == 2:
        one = jax.random.randint(rng, (), max(1, total - bound), min(bound, total - 1) + 1)
        return jnp.stack([one, total - one])
    tallies = jnp.asarray(split_up(amount, total, bound, lean), jnp.int32)
    twos = (amount - 1) // 2
    donor, sink = tallies[1:1 + 2 * twos:2], tallies[2:2 + 2 * twos:2]
    room = jnp.minimum(donor - 1, bound - sink)
    shifted = jax.random.randint(jax.random.fold_in(rng, 1), (twos,), 0, 1 << 20) % (room + 1)
    tallies = tallies.at[1:1 + 2 * twos:2].set(donor - shifted).at[2:2 + 2 * twos:2].set(sink + shifted)
    return tallies[jax.random.permutation(jax.random.fold_in(rng, 2), amount)]


def gaussian(stream_key, shape, width, reach, cuts=(), kind=jnp.bfloat16):
    values = jax.random.normal(stream_key, shape, jnp.float32) * width
    if len(cuts) > 0:
        values = levels(stream_key, shape, cuts, -0.22, 0.18) * values
    return jnp.clip(values, min=-reach, max=reach).astype(kind)


def setup_inputs(seed: int = 0) -> dict:
    streams_of = jax.random.split(jax.random.key(seed), 7)
    tokens_in = gaussian(streams_of[0], (BATCH, SEQUENCE_LENGTH, D), 1.0, 6.0, ((0, 16), (1, 32)))
    queries = draw_queries(jax.random.fold_in(streams_of[6], 71), 0)
    values_in = gaussian(streams_of[2], (BATCH, SEQUENCE_LENGTH, KEY_FEATURES), 1.0, 6.0, ((0, 16), (1, 32)))
    key_weight = gaussian(streams_of[3], (D, KEY_FEATURES), D ** -0.5, 0.109375, ((0, 16), (1, 32)))
    out_grad = gaussian(streams_of[4], (BATCH, SEQUENCE_LENGTH, QW), 1.0, 6.0, ((0, 16), (1, 32)))
    doc_ids = jax.vmap(lambda own: jnp.searchsorted(jnp.cumsum(ragged(own, DOCS, SEQUENCE_LENGTH, DOC_MOST, 1)), jnp.arange(SEQUENCE_LENGTH), side="right"))(jax.random.split(streams_of[5], BATCH)).reshape((BATCH, SEQUENCE_LENGTH)).astype(jnp.int32)
    return {"tokens_in": tokens_in, "queries": queries, "values_in": values_in, "key_weight": key_weight, "out_grad": out_grad, "doc_ids": doc_ids}


rope_base = 150000.0
masked_score = -1.0e30


def rope_tables(positions):
    half_dim = HEAD_SIZE // 2
    exponent = jnp.arange(half_dim, dtype=jnp.float32) * (-2.0 / HEAD_SIZE)
    inverse_freq = jnp.power(jnp.float32(rope_base), exponent)
    angles = positions.astype(jnp.float32)[:, None] * inverse_freq[None, :]
    return jnp.cos(angles)[:, None, :], jnp.sin(angles)[:, None, :]


def apply_rotary(tensor, cosine_table, sine_table):
    half_dim = HEAD_SIZE // 2
    first_half = tensor[..., :half_dim]
    second_half = tensor[..., half_dim:]
    return jnp.concatenate([first_half * cosine_table - second_half * sine_table, second_half * cosine_table + first_half * sine_table], axis=-1)


def invert_rotary(tensor, cosine_table, sine_table):
    half_dim = HEAD_SIZE // 2
    first_half = tensor[..., :half_dim]
    second_half = tensor[..., half_dim:]
    return jnp.concatenate([first_half * cosine_table + second_half * sine_table, second_half * cosine_table - first_half * sine_table], axis=-1)


def mixed(form, left_side, right_side):
    return jnp.einsum(form, left_side.astype(jnp.float32), right_side.astype(jnp.float32), precision=lax.Precision.HIGHEST)


def band_block(query_row_tensor, gradient_rows, key_row_tensor, value_row_tensor, query_docs, key_docs):
    row_number_total = query_row_tensor.shape[0]
    key_window_span = key_row_tensor.shape[0]
    query_group_width = QUERY_HEAD_COUNT // KEY_VALUE_HEADS
    score_scale = HEAD_SIZE ** -0.5
    query_head_tensor = query_row_tensor.reshape(row_number_total, KEY_VALUE_HEADS, query_group_width, HEAD_SIZE)
    gradient_heads = gradient_rows.reshape(row_number_total, KEY_VALUE_HEADS, query_group_width, HEAD_SIZE)
    key_head_tensor = key_row_tensor.reshape(key_window_span, KEY_VALUE_HEADS, HEAD_SIZE)
    value_head_tensor = value_row_tensor.reshape(key_window_span, KEY_VALUE_HEADS, HEAD_SIZE)
    scores = mixed("rkgd,ckd->kgrc", query_head_tensor, key_head_tensor) * score_scale
    distance = jnp.arange(row_number_total, dtype=jnp.int32)[:, None] + WINDOW_LENGTH - jnp.arange(key_window_span, dtype=jnp.int32)[None, :]
    allowed = (distance >= 0) & (distance <= WINDOW_LENGTH) & (query_docs[:, None] == key_docs[None, :])
    scores = jnp.where(allowed[None, None], scores, masked_score)
    row_max = jnp.max(scores, axis=-1, keepdims=True)
    weights = jnp.exp(scores - row_max)
    prob_rows = weights / jnp.sum(weights, axis=-1, keepdims=True)
    probs_low = prob_rows.astype(jnp.bfloat16)
    attn_out = mixed("kgrc,ckd->rkgd", probs_low, value_head_tensor)
    row_delta = jnp.sum(gradient_heads.astype(jnp.float32) * attn_out, axis=-1)
    value_part = mixed("kgrc,rkgd->ckd", probs_low, gradient_heads)
    prob_grad = mixed("rkgd,ckd->kgrc", gradient_heads, value_head_tensor)
    score_grad = prob_rows * (prob_grad - jnp.transpose(row_delta, (1, 2, 0))[..., None])
    score_low = score_grad.astype(jnp.bfloat16)
    query_part = mixed("kgrc,ckd->rkgd", score_low, key_head_tensor) * score_scale
    key_part = mixed("kgrc,rkgd->ckd", score_low, query_head_tensor) * score_scale
    return query_part.reshape(row_number_total, QUERY_HEAD_COUNT * HEAD_SIZE), key_part.reshape(key_window_span, KEY_FEATURES), value_part.reshape(key_window_span, KEY_FEATURES)


def reference(tokens_in, queries, values_in, key_weight, out_grad, doc_ids):
    positions = jnp.arange(SEQUENCE_LENGTH, dtype=jnp.int32)
    cosine_table, sine_table = rope_tables(positions)
    block_count = SEQUENCE_LENGTH // WINDOW_LENGTH

    def one_sequence(weight_total, sequence_items):
        inputs, query_row_tensor, value_row_tensor, gradient_rows, doc_row = sequence_items
        key_linear_output = jnp.dot(inputs, key_weight, preferred_element_type=jnp.float32)
        keys_reduced_precision = apply_rotary(key_linear_output.reshape(SEQUENCE_LENGTH, KEY_VALUE_HEADS, HEAD_SIZE), cosine_table, sine_table).reshape(SEQUENCE_LENGTH, KEY_FEATURES).astype(jnp.bfloat16)
        band_keys = jnp.concatenate([jnp.zeros((WINDOW_LENGTH, KEY_FEATURES), jnp.bfloat16), keys_reduced_precision], axis=0)
        band_values = jnp.concatenate([jnp.zeros((WINDOW_LENGTH, KEY_FEATURES), jnp.bfloat16), value_row_tensor], axis=0)
        band_docs = jnp.concatenate([jnp.full((WINDOW_LENGTH,), -1, jnp.int32), doc_row.astype(jnp.int32)], axis=0)

        def one_block(carried, block_index):
            key_full_gathered, value_total = carried
            offset = (block_index * WINDOW_LENGTH).astype(jnp.int32)
            query_part, key_part, value_part = band_block(
                lax.dynamic_slice_in_dim(query_row_tensor, offset, WINDOW_LENGTH),
                lax.dynamic_slice_in_dim(gradient_rows, offset, WINDOW_LENGTH),
                lax.dynamic_slice_in_dim(band_keys, offset, 2 * WINDOW_LENGTH),
                lax.dynamic_slice_in_dim(band_values, offset, 2 * WINDOW_LENGTH),
                lax.dynamic_slice_in_dim(band_docs, offset + WINDOW_LENGTH, WINDOW_LENGTH),
                lax.dynamic_slice_in_dim(band_docs, offset, 2 * WINDOW_LENGTH))
            key_full_gathered = lax.dynamic_update_slice_in_dim(key_full_gathered, lax.dynamic_slice_in_dim(key_full_gathered, offset, 2 * WINDOW_LENGTH) + key_part, offset, 0)
            value_total = lax.dynamic_update_slice_in_dim(value_total, lax.dynamic_slice_in_dim(value_total, offset, 2 * WINDOW_LENGTH) + value_part, offset, 0)
            return (key_full_gathered, value_total), query_part.astype(jnp.bfloat16)

        start_totals = (jnp.zeros((SEQUENCE_LENGTH + WINDOW_LENGTH, KEY_FEATURES), jnp.float32), jnp.zeros((SEQUENCE_LENGTH + WINDOW_LENGTH, KEY_FEATURES), jnp.float32))
        (key_full_gathered, value_total), query_blocks = lax.scan(one_block, start_totals, jnp.arange(block_count, dtype=jnp.int32))
        query_grad = query_blocks.reshape(SEQUENCE_LENGTH, QUERY_HEAD_COUNT * HEAD_SIZE)
        value_grad = value_total[WINDOW_LENGTH:].astype(jnp.bfloat16)
        key_linear_gradient = invert_rotary(key_full_gathered[WINDOW_LENGTH:].reshape(SEQUENCE_LENGTH, KEY_VALUE_HEADS, HEAD_SIZE), cosine_table, sine_table).reshape(SEQUENCE_LENGTH, KEY_FEATURES).astype(jnp.bfloat16)
        input_grad = lax.dot_general(key_linear_gradient, key_weight, (((1,), (1,)), ((), ())), preferred_element_type=jnp.float32).astype(jnp.bfloat16)
        weight_total = weight_total + lax.dot_general(inputs, key_linear_gradient, (((0,), (0,)), ((), ())), preferred_element_type=jnp.float32)
        return weight_total, (query_grad, value_grad, input_grad)

    weight_grad, outputs = lax.scan(one_sequence, jnp.zeros((D, KEY_FEATURES), jnp.float32), (tokens_in, queries, values_in, out_grad, doc_ids))
    query_grad, value_grad, input_grad = outputs
    return (query_grad, value_grad, input_grad, weight_grad)
```

```python
import jax
import jax.numpy as jnp
from jax import lax
from jax.experimental import pallas as pl
from jax.experimental.pallas import tpu as pltpu
from jax.sharding import Mesh
from jax.sharding import PartitionSpec as P

QUERY_HEADS = 32
KV_HEADS = 4
HEAD = 64
WINDOW = 128
KEYF = 256
GROUP = QUERY_HEADS // KV_HEADS
ROWS = 64
rope_base = 150000.0
masked_score = -1e30
bf16 = jnp.bfloat16
f32 = jnp.float32

DP = ("zl", "y")
CTX = ("zh", "x", "core")
Z = ("zl", "zh")


def nt(a, b):
    return lax.dot_general(a, b, (((1,), (1,)), ((), ())), preferred_element_type=f32)


def nn(a, b):
    return lax.dot_general(a, b, (((1,), (0,)), ((), ())), preferred_element_type=f32)


def tn(a, b):
    return lax.dot_general(a, b, (((0,), (0,)), ((), ())), preferred_element_type=f32)


def swap_halves(x):
    lane = lax.broadcasted_iota(jnp.int32, x.shape, 1)
    width = x.shape[1]
    return jnp.where(lane % HEAD < HEAD // 2, pltpu.roll(x, width - HEAD // 2, 1), pltpu.roll(x, HEAD // 2, 1))


def project_kernel(tokens_ref, weight_ref, cos_ref, sin_ref, keys_ref):
    linear = nt(tokens_ref[...], weight_ref[...])
    keys_ref[...] = (linear * cos_ref[...] + swap_halves(linear) * sin_ref[...]).astype(bf16)


def doubled(tile, parity):
    wide = tile.astype(f32)
    lane = lax.broadcasted_iota(jnp.int32, wide.shape, 1)
    return jnp.where(lane // HEAD == parity, wide, pltpu.roll(wide, HEAD, 1))


def attention_kernel(
    q_ref, g_ref, k_ref, v_ref, hk_ref, hv_ref, qd_ref, kd_ref, dq_ref, dk_ref, dv_ref,
    bias_ref, kk_ref, vv_ref, dka_ref, dva_ref,
):
    step = pl.program_id(0)
    parity = step % 2
    rows = q_ref.shape[0]
    span = ROWS + WINDOW
    lanes = GROUP * ROWS
    blocks = rows // ROWS

    @pl.when(step == 0)
    def _():
        key_at = lax.broadcasted_iota(jnp.int32, (span, lanes), 0)
        query_at = lax.broadcasted_iota(jnp.int32, (span, lanes), 1) % ROWS
        distance = query_at + WINDOW - key_at
        near = (distance >= 0) & (distance <= WINDOW)
        for b in range(blocks):
            same = kd_ref[b * ROWS : b * ROWS + span, :] == qd_ref[b]
            bias_ref[b] = jnp.where(near & same, 0.0, masked_score)

    kk_ref[:WINDOW, :] = (doubled(hk_ref[...], parity) * 0.125).astype(bf16)
    kk_ref[WINDOW:, :] = (doubled(k_ref[...], parity) * 0.125).astype(bf16)
    vv_ref[:WINDOW, :] = doubled(hv_ref[...], parity).astype(bf16)
    vv_ref[WINDOW:, :] = doubled(v_ref[...], parity).astype(bf16)
    dka_ref[...] = jnp.zeros_like(dka_ref)
    dva_ref[...] = jnp.zeros_like(dva_ref)
    lane = lax.broadcasted_iota(jnp.int32, (ROWS, 2 * HEAD), 1)
    low = jnp.where(lane < HEAD, 1.0, 0.0).astype(bf16)
    high = jnp.where(lane < HEAD, 0.0, 1.0).astype(bf16)

    def stacked(ref, b):
        parts = []
        for p in range(GROUP // 2):
            pair = ref[b * ROWS : (b + 1) * ROWS, p * 2 * HEAD : (p + 1) * 2 * HEAD]
            parts += [pair * low, pair * high]
        return jnp.concatenate(parts, axis=0)

    for b in range(blocks):
        band = slice(b * ROWS, b * ROWS + span)
        keys = kk_ref[band, :]
        values = vv_ref[band, :]
        qs = stacked(q_ref, b)
        gs = stacked(g_ref, b)
        scores = nt(keys, qs) + bias_ref[b]
        weights = jnp.exp(scores - jnp.max(scores, axis=0, keepdims=True))
        probs = weights * (1.0 / jnp.sum(weights, axis=0, keepdims=True))
        probs_low = probs.astype(bf16)
        prob_grad = nt(values, gs)
        delta = jnp.sum(probs_low.astype(f32) * prob_grad, axis=0, keepdims=True)
        score_low = (probs * (prob_grad - delta)).astype(bf16)
        dva_ref[band, :] += nn(probs_low, gs)
        dka_ref[band, :] += nn(score_low, qs)
        dq = tn(score_low, keys)
        for p in range(GROUP // 2):
            top = dq[2 * p * ROWS : (2 * p + 1) * ROWS]
            bottom = dq[(2 * p + 1) * ROWS : (2 * p + 2) * ROWS]
            dq_ref[b * ROWS : (b + 1) * ROWS, p * 2 * HEAD : (p + 1) * 2 * HEAD] = jnp.where(
                lane < HEAD, top, bottom
            ).astype(bf16)

    wide = lax.broadcasted_iota(jnp.int32, dka_ref.shape, 1)
    mine = wide // HEAD == parity
    dk = dka_ref[...] * 0.125
    dv = dva_ref[...]
    dk_ref[...] = jnp.where(mine, dk + pltpu.roll(dk, HEAD, 1), dk_ref[...])
    dv_ref[...] = jnp.where(mine, dv + pltpu.roll(dv, HEAD, 1), dv_ref[...])


def tail_kernel(
    dk_ref, dv_ref, inc_ref, cos_ref, sin_ref, tokens_ref, weight_ref, order_ref,
    vg_ref, ig_ref, own_ref, send_ref,
):
    rows = tokens_ref.shape[0]
    edge = rows - WINDOW
    vg_ref[:edge, :] = dv_ref[WINDOW : WINDOW + edge, :].astype(bf16)
    vg_ref[edge:, :] = (dv_ref[WINDOW + edge :, :] + inc_ref[:, KEYF:]).astype(bf16)
    dk = jnp.concatenate(
        [dk_ref[WINDOW : WINDOW + edge, :], dk_ref[WINDOW + edge :, :] + inc_ref[:, :KEYF]], axis=0
    )
    lin = (dk * cos_ref[...] - swap_halves(dk) * sin_ref[...]).astype(bf16)
    ordered = nt(order_ref[...], lin).astype(bf16)
    half = KEYF // 2
    own_ref[...] = nn(ordered[:half], tokens_ref[...])
    send_ref[...] = nn(ordered[half:], tokens_ref[...]).astype(bf16)
    ig_ref[...] = nn(lin, weight_ref[...]).astype(bf16)


def spread(x, axes):
    peers = lax.axis_size(axes)
    return lax.all_to_all(jnp.broadcast_to(x[None], (peers,) + x.shape), axes, 0, 0, tiled=True)


def exchanged(x, axis):
    return lax.ppermute(x, axis, [(0, 1), (1, 0)])


def gathered_weight(block):
    width = block.shape[0]
    sub = block.shape[1]
    zl, y, zh, x = (lax.axis_size(a) for a in ("zl", "y", "zh", "x"))
    along_z = spread(block.T, Z)
    along_y = spread(along_z, "y")
    rows = along_y.reshape(y, zl, zh, sub, width).transpose(2, 3, 1, 0, 4).reshape(zh, sub, zl * y * width)
    along_x = lax.all_gather(rows, "x", axis=0)
    other = exchanged(along_x, "core")
    first = lax.axis_index("core") == 0
    pair = jnp.stack([jnp.where(first, along_x, other), jnp.where(first, other, along_x)], axis=2)
    return pair.transpose(1, 0, 2, 3, 4).reshape(zh * x * 2 * sub, zl * y * width)


def scattered_gradient(own, send, width, sub):
    zl, y, zh, x = (lax.axis_size(a) for a in ("zl", "y", "zh", "x"))
    both = (own + exchanged(send, "core").astype(f32)).astype(bf16)
    both = both.reshape(x, zh, sub, zl * y * width)
    over_x = jnp.sum(lax.all_to_all(both, "x", 0, 0, tiled=True).astype(f32), axis=0).astype(bf16)
    over_x = over_x.reshape(zh, sub, zl, y, width).transpose(3, 2, 0, 1, 4).reshape(y, zl * zh, sub, width)
    over_y = jnp.sum(lax.all_to_all(over_x, "y", 0, 0, tiled=True).astype(f32), axis=0).astype(bf16)
    return jnp.sum(lax.all_to_all(over_y, Z, 0, 0, tiled=True).astype(f32), axis=0)


def per_device(tokens_in, queries, values_in, key_weight, out_grad, doc_ids):
    rows = tokens_in.shape[1]
    dim = tokens_in.shape[2]
    width, sub = key_weight.shape
    tokens, q, g, v = tokens_in[0], queries[0], out_grad[0], values_in[0]
    blocks = rows // ROWS
    peers = lax.axis_size(CTX)
    position = lax.axis_index(CTX)
    first_row = position * rows

    exponent = jnp.arange(HEAD // 2, dtype=f32) * (-2.0 / HEAD)
    inverse_freq = jnp.power(f32(rope_base), exponent)
    angles = (first_row + jnp.arange(rows, dtype=jnp.int32)).astype(f32)[:, None] * inverse_freq[None, :]
    cosine, sine = jnp.cos(angles), jnp.sin(angles)
    cos_table = jnp.tile(cosine, (1, 2 * KV_HEADS))
    sin_table = jnp.tile(jnp.concatenate([-sine, sine], axis=1), (1, KV_HEADS))

    padded_docs = jnp.concatenate([jnp.full((WINDOW,), -1, jnp.int32), doc_ids[0]])
    band_docs = lax.dynamic_slice_in_dim(padded_docs, first_row, rows + WINDOW)
    query_docs = jnp.tile(band_docs[WINDOW:].reshape(blocks, 1, ROWS), (1, 1, GROUP))
    key_docs = band_docs[:, None]

    core = lax.axis_index("core")
    zh, x = lax.axis_size("zh"), lax.axis_size("x")
    dest = jnp.arange(KEYF, dtype=jnp.int32)
    rel, dest_x, dest_zh, dest_j = dest // 128, dest // 32 % 4, dest // 8 % 4, dest % 8
    source = dest_zh * 64 + dest_x * 16 + (rel ^ core) * 8 + dest_j
    order = (source[:, None] == jnp.arange(KEYF, dtype=jnp.int32)[None, :]).astype(bf16)

    weight = gathered_weight(key_weight)

    params = pltpu.CompilerParams(vmem_limit_bytes=40 << 20)
    keys = pl.pallas_call(
        project_kernel,
        out_shape=jax.ShapeDtypeStruct((rows, KEYF), bf16),
        compiler_params=params,
        name="project",
    )(tokens, weight, cos_table, sin_table)

    along = [(i, i + 1) for i in range(peers - 1)]
    back = [(i + 1, i) for i in range(peers - 1)]
    halo = lax.ppermute(jnp.concatenate([keys[rows - WINDOW :], v[rows - WINDOW :]], axis=1), CTX, along)

    span = ROWS + WINDOW
    dq, dk, dv = pl.pallas_call(
        attention_kernel,
        grid=(KV_HEADS,),
        in_specs=[
            pl.BlockSpec((rows, GROUP * HEAD), lambda k: (0, k)),
            pl.BlockSpec((rows, GROUP * HEAD), lambda k: (0, k)),
            pl.BlockSpec((rows, 2 * HEAD), lambda k: (0, k // 2)),
            pl.BlockSpec((rows, 2 * HEAD), lambda k: (0, k // 2)),
            pl.BlockSpec((WINDOW, 2 * HEAD), lambda k: (0, k // 2)),
            pl.BlockSpec((WINDOW, 2 * HEAD), lambda k: (0, 2 + k // 2)),
            pl.BlockSpec((blocks, 1, GROUP * ROWS), lambda k: (0, 0, 0)),
            pl.BlockSpec((rows + WINDOW, 1), lambda k: (0, 0)),
        ],
        out_specs=[
            pl.BlockSpec((rows, GROUP * HEAD), lambda k: (0, k)),
            pl.BlockSpec((rows + WINDOW, 2 * HEAD), lambda k: (0, k // 2)),
            pl.BlockSpec((rows + WINDOW, 2 * HEAD), lambda k: (0, k // 2)),
        ],
        out_shape=[
            jax.ShapeDtypeStruct((rows, QUERY_HEADS * HEAD), bf16),
            jax.ShapeDtypeStruct((rows + WINDOW, KEYF), f32),
            jax.ShapeDtypeStruct((rows + WINDOW, KEYF), f32),
        ],
        scratch_shapes=[
            pltpu.VMEM((blocks, span, GROUP * ROWS), f32),
            pltpu.VMEM((rows + WINDOW, 2 * HEAD), bf16),
            pltpu.VMEM((rows + WINDOW, 2 * HEAD), bf16),
            pltpu.VMEM((rows + WINDOW, 2 * HEAD), f32),
            pltpu.VMEM((rows + WINDOW, 2 * HEAD), f32),
        ],
        compiler_params=params,
        name="band_attention",
    )(q, g, keys, v, halo, halo, query_docs, key_docs)

    incoming = lax.ppermute(jnp.concatenate([dk[:WINDOW], dv[:WINDOW]], axis=1), CTX, back)

    value_grad, input_grad, own, send = pl.pallas_call(
        tail_kernel,
        out_shape=[
            jax.ShapeDtypeStruct((rows, KEYF), bf16),
            jax.ShapeDtypeStruct((rows, dim), bf16),
            jax.ShapeDtypeStruct((KEYF // 2, dim), f32),
            jax.ShapeDtypeStruct((KEYF // 2, dim), bf16),
        ],
        compiler_params=params,
        name="tail",
    )(dk, dv, incoming, cos_table, sin_table, tokens, weight, order)

    weight_grad = scattered_gradient(own, send, width, sub).T
    return dq[None], value_grad[None], input_grad[None], weight_grad


def solution(mesh):
    fine = Mesh(mesh.devices.reshape(4, 4, 4, 4, 2), ("zl", "y", "zh", "x", "core"))
    rows = P(DP, CTX, None)
    square = P(DP, CTX)
    return jax.shard_map(
        per_device,
        mesh=fine,
        in_specs=(rows, rows, rows, square, rows, P(DP, None)),
        out_specs=(rows, rows, rows, square),
        check_vma=False,
    )
```

```python
import jax
import jax.numpy as jnp
from jax import lax
from jax.experimental import pallas as pl
from jax.experimental.pallas import tpu as pltpu
from jax.sharding import Mesh
from jax.sharding import PartitionSpec as P

QUERY_HEADS = 32
KV_HEADS = 4
HEAD = 64
WINDOW = 128
KEYF = 256
GROUP = QUERY_HEADS // KV_HEADS
ROWS = 64
rope_base = 150000.0
masked_score = -1e30
bf16 = jnp.bfloat16
f32 = jnp.float32

DP = ("zl", "y")
CTX = ("zh", "x", "core")
Z = ("zl", "zh")
YX = ("y", "x")


def nt(a, b):
    return lax.dot_general(a, b, (((1,), (1,)), ((), ())), preferred_element_type=f32)


def nn(a, b):
    return lax.dot_general(a, b, (((1,), (0,)), ((), ())), preferred_element_type=f32)


def tn(a, b):
    return lax.dot_general(a, b, (((0,), (0,)), ((), ())), preferred_element_type=f32)


def swap_halves(x):
    lane = lax.broadcasted_iota(jnp.int32, x.shape, 1)
    width = x.shape[1]
    return jnp.where(lane % HEAD < HEAD // 2, pltpu.roll(x, width - HEAD // 2, 1), pltpu.roll(x, HEAD // 2, 1))


def project_kernel(tokens_ref, weight_ref, v_ref, cos_ref, sin_ref, keys_ref, edge_ref, packed_ref):
    parts, rows, wide = packed_ref.shape
    width = wide // parts
    linear = jnp.zeros((rows, KEYF), f32)
    for y in range(parts):
        for zl in range(parts):
            at = (zl * parts + y) * width
            packed_ref[y, :, zl * width : (zl + 1) * width] = tokens_ref[:, at : at + width]
        linear += nt(packed_ref[y], weight_ref[y])
    keys = (linear * cos_ref[...] + swap_halves(linear) * sin_ref[...]).astype(bf16)
    keys_ref[...] = keys
    edge_ref[0] = keys[rows - WINDOW :]
    edge_ref[1] = v_ref[rows - WINDOW :, :]


def attention_kernel(
    q_ref, g_ref, k_ref, v_ref, edge_ref, qd_ref, kd_ref,
    dq_ref, dk_ref, dv_ref, out_edge_ref,
    bias_ref, kk_ref, vv_ref, dka_ref, dva_ref,
):
    rows = q_ref.shape[0]
    span = ROWS + WINDOW
    lanes = GROUP * ROWS
    blocks = rows // ROWS

    @pl.when(pl.program_id(0) == 0)
    def _():
        key_at = lax.broadcasted_iota(jnp.int32, (span, lanes), 0)
        query_at = lax.broadcasted_iota(jnp.int32, (span, lanes), 1) % ROWS
        distance = query_at + WINDOW - key_at
        near = (distance >= 0) & (distance <= WINDOW)
        for b in range(blocks):
            same = kd_ref[b * ROWS : b * ROWS + span, :] == qd_ref[b]
            bias_ref[b] = jnp.where(near & same, 0.0, masked_score)

    lane = lax.broadcasted_iota(jnp.int32, (ROWS, 2 * HEAD), 1)
    low = jnp.where(lane < HEAD, 1.0, 0.0).astype(bf16)
    high = jnp.where(lane < HEAD, 0.0, 1.0).astype(bf16)

    def doubled(tile, head, scale):
        wide = tile.astype(f32) * scale
        at = lax.broadcasted_iota(jnp.int32, wide.shape, 1)
        return jnp.where(at // HEAD == head, wide, pltpu.roll(wide, HEAD, 1)).astype(bf16)

    def stacked(ref, b, head):
        parts = []
        for p in range(GROUP // 2):
            at = (head * GROUP // 2 + p) * 2 * HEAD
            pair = ref[b * ROWS : (b + 1) * ROWS, at : at + 2 * HEAD]
            parts += [pair * low, pair * high]
        return jnp.concatenate(parts, axis=0)

    for head in range(2):
        kk_ref[:WINDOW, :] = doubled(edge_ref[0], head, 0.125)
        kk_ref[WINDOW:, :] = doubled(k_ref[...], head, 0.125)
        vv_ref[:WINDOW, :] = doubled(edge_ref[1], head, 1.0)
        vv_ref[WINDOW:, :] = doubled(v_ref[...], head, 1.0)
        dka_ref[head] = jnp.zeros_like(dka_ref[head])
        dva_ref[head] = jnp.zeros_like(dva_ref[head])
        for b in range(blocks):
            band = slice(b * ROWS, b * ROWS + span)
            keys = kk_ref[band, :]
            values = vv_ref[band, :]
            qs = stacked(q_ref, b, head)
            gs = stacked(g_ref, b, head)
            scores = nt(keys, qs) + bias_ref[b]
            weights = jnp.exp(scores - jnp.max(scores, axis=0, keepdims=True))
            probs = weights * (1.0 / jnp.sum(weights, axis=0, keepdims=True))
            probs_low = probs.astype(bf16)
            prob_grad = nt(values, gs)
            delta = jnp.sum(probs_low.astype(f32) * prob_grad, axis=0, keepdims=True)
            score_low = (probs * (prob_grad - delta)).astype(bf16)
            dva_ref[head, band, :] += nn(probs_low, gs)
            dka_ref[head, band, :] += nn(score_low, qs)
            dq = tn(score_low, keys)
            for p in range(GROUP // 2):
                at = (head * GROUP // 2 + p) * 2 * HEAD
                top = dq[2 * p * ROWS : (2 * p + 1) * ROWS]
                bottom = dq[(2 * p + 1) * ROWS : (2 * p + 2) * ROWS]
                dq_ref[b * ROWS : (b + 1) * ROWS, at : at + 2 * HEAD] = jnp.where(
                    lane < HEAD, top, bottom
                ).astype(bf16)

    def joined(ref):
        first, second = ref[0], ref[1]
        at = lax.broadcasted_iota(jnp.int32, first.shape, 1)
        first = first + pltpu.roll(first, HEAD, 1)
        second = second + pltpu.roll(second, HEAD, 1)
        return jnp.where(at < HEAD, first, second)

    dk = joined(dka_ref) * 0.125
    dv = joined(dva_ref)
    out_edge_ref[0] = dk[:WINDOW].astype(bf16)
    out_edge_ref[1] = dv[:WINDOW].astype(bf16)
    dk_ref[...] = dk[WINDOW:]
    dv_ref[...] = dv[WINDOW:]


def tail_kernel(
    dk_ref, dv_ref, edge_ref, cos_ref, sin_ref, packed_ref, weight_ref, order_ref,
    vg_ref, ig_ref, own_ref, send_ref,
):
    parts, rows, wide = packed_ref.shape
    width = wide // parts
    start = rows - WINDOW
    vg_ref[:start, :] = dv_ref[:start, :].astype(bf16)
    vg_ref[start:, :] = (dv_ref[start:, :] + edge_ref[1].astype(f32)).astype(bf16)
    dk = jnp.concatenate([dk_ref[:start, :], dk_ref[start:, :] + edge_ref[0].astype(f32)], axis=0)
    lin = (dk * cos_ref[...] - swap_halves(dk) * sin_ref[...]).astype(bf16)
    ordered = nt(order_ref[...], lin).astype(bf16)
    half = KEYF // 2
    for y in range(parts):
        own_ref[y] = nn(ordered[:half], packed_ref[y])
        send_ref[y] = nn(ordered[half:], packed_ref[y]).astype(bf16)
        part = nn(lin, weight_ref[y]).astype(bf16)
        for zl in range(parts):
            at = (zl * parts + y) * width
            ig_ref[:, at : at + width] = part[:, zl * width : (zl + 1) * width]


def spread(x, axes):
    peers = lax.axis_size(axes)
    return lax.all_to_all(jnp.broadcast_to(x[None], (peers,) + x.shape), axes, 0, 0, tiled=True)


def exchanged(x, axis):
    return lax.ppermute(x, axis, [(0, 1), (1, 0)])


def gathered_weight(block):
    width, sub = block.shape
    zl, y, zh, x = (lax.axis_size(a) for a in ("zl", "y", "zh", "x"))
    along_z = spread(block.T, Z).reshape(zl, zh, sub, width)
    rows = along_z.transpose(1, 2, 0, 3).reshape(zh * sub, zl * width)
    mine = spread(rows, YX)
    other = exchanged(mine, "core")
    first = lax.axis_index("core") == 0
    pair = jnp.stack([jnp.where(first, mine, other), jnp.where(first, other, mine)])
    pair = pair.reshape(2, y, x, zh, sub, zl * width).transpose(1, 3, 2, 0, 4, 5)
    return pair.reshape(y, zh * x * 2 * sub, zl * width)


def summed(x, axes):
    return jnp.sum(lax.all_to_all(x, axes, 0, 0, tiled=True).astype(f32), axis=0)


def scattered_gradient(own, send, width, sub):
    zl, y, zh, x = (lax.axis_size(a) for a in ("zl", "y", "zh", "x"))
    both = (own + exchanged(send, "core").astype(f32)).astype(bf16)
    over_yx = summed(both.reshape(y * x, zh * sub, zl * width), YX).astype(bf16)
    over_yx = over_yx.reshape(zh, sub, zl, width).transpose(2, 0, 1, 3)
    return summed(over_yx.reshape(zl * zh, sub, width), Z)


def per_device(tokens_in, queries, values_in, key_weight, out_grad, doc_ids):
    rows = tokens_in.shape[1]
    dim = tokens_in.shape[2]
    width, sub = key_weight.shape
    tokens, q, g, v = tokens_in[0], queries[0], out_grad[0], values_in[0]
    q = pltpu.with_memory_space_constraint(q, pltpu.HBM)
    g = pltpu.with_memory_space_constraint(g, pltpu.HBM)
    blocks = rows // ROWS
    parts = lax.axis_size("y")
    peers = lax.axis_size(CTX)
    position = lax.axis_index(CTX)
    first_row = position * rows

    exponent = jnp.arange(HEAD // 2, dtype=f32) * (-2.0 / HEAD)
    inverse_freq = jnp.power(f32(rope_base), exponent)
    angles = (first_row + jnp.arange(rows, dtype=jnp.int32)).astype(f32)[:, None] * inverse_freq[None, :]
    cosine, sine = jnp.cos(angles), jnp.sin(angles)
    cos_table = jnp.tile(cosine, (1, 2 * KV_HEADS))
    sin_table = jnp.tile(jnp.concatenate([-sine, sine], axis=1), (1, KV_HEADS))

    padded_docs = jnp.concatenate([jnp.full((WINDOW,), -1, jnp.int32), doc_ids[0]])
    band_docs = lax.dynamic_slice_in_dim(padded_docs, first_row, rows + WINDOW)
    query_docs = jnp.tile(band_docs[WINDOW:].reshape(blocks, 1, ROWS), (1, 1, GROUP))
    key_docs = band_docs[:, None]

    core = lax.axis_index("core")
    dest = jnp.arange(KEYF, dtype=jnp.int32)
    rel, dest_x, dest_zh, dest_j = dest // 128, dest // 32 % 4, dest // 8 % 4, dest % 8
    source = dest_zh * 64 + dest_x * 16 + (rel ^ core) * 8 + dest_j
    order = (source[:, None] == jnp.arange(KEYF, dtype=jnp.int32)[None, :]).astype(bf16)

    weight = gathered_weight(key_weight)

    params = pltpu.CompilerParams(vmem_limit_bytes=24 << 20)
    keys, edge, packed = pl.pallas_call(
        project_kernel,
        out_shape=[
            jax.ShapeDtypeStruct((rows, KEYF), bf16),
            jax.ShapeDtypeStruct((2, WINDOW, KEYF), bf16),
            jax.ShapeDtypeStruct((parts, rows, dim // parts), bf16),
        ],
        compiler_params=params,
        name="project",
    )(tokens, weight, v, cos_table, sin_table)

    along = [(i, i + 1) for i in range(peers - 1)]
    back = [(i + 1, i) for i in range(peers - 1)]
    prior = lax.ppermute(edge, CTX, along)

    span = ROWS + WINDOW
    pair = 2 * HEAD
    heads = pl.BlockSpec((rows, 2 * GROUP * HEAD), lambda k: (0, k))
    own_tile = pl.BlockSpec((rows, pair), lambda k: (0, k))
    edge_tile = pl.BlockSpec((2, WINDOW, pair), lambda k: (0, 0, k))
    dq, dk, dv, out_edge = pl.pallas_call(
        attention_kernel,
        grid=(KV_HEADS // 2,),
        in_specs=[
            heads,
            heads,
            own_tile,
            own_tile,
            edge_tile,
            pl.BlockSpec((blocks, 1, GROUP * ROWS), lambda k: (0, 0, 0)),
            pl.BlockSpec((rows + WINDOW, 1), lambda k: (0, 0)),
        ],
        out_specs=[heads, own_tile, own_tile, edge_tile],
        out_shape=[
            jax.ShapeDtypeStruct((rows, QUERY_HEADS * HEAD), bf16),
            jax.ShapeDtypeStruct((rows, KEYF), f32),
            jax.ShapeDtypeStruct((rows, KEYF), f32),
            jax.ShapeDtypeStruct((2, WINDOW, KEYF), bf16),
        ],
        scratch_shapes=[
            pltpu.VMEM((blocks, span, GROUP * ROWS), f32),
            pltpu.VMEM((rows + WINDOW, pair), bf16),
            pltpu.VMEM((rows + WINDOW, pair), bf16),
            pltpu.VMEM((2, rows + WINDOW, pair), f32),
            pltpu.VMEM((2, rows + WINDOW, pair), f32),
        ],
        compiler_params=params,
        name="band_attention",
    )(q, g, keys, v, prior, query_docs, key_docs)

    incoming = lax.ppermute(out_edge, CTX, back)

    value_grad, input_grad, own, send = pl.pallas_call(
        tail_kernel,
        out_shape=[
            jax.ShapeDtypeStruct((rows, KEYF), bf16),
            jax.ShapeDtypeStruct((rows, dim), bf16),
            jax.ShapeDtypeStruct((parts, KEYF // 2, dim // parts), f32),
            jax.ShapeDtypeStruct((parts, KEYF // 2, dim // parts), bf16),
        ],
        compiler_params=params,
        name="tail",
    )(dk, dv, incoming, cos_table, sin_table, packed, weight, order)

    weight_grad = scattered_gradient(own, send, width, sub).T
    return dq[None], value_grad[None], input_grad[None], weight_grad


def solution(mesh):
    fine = Mesh(mesh.devices.reshape(4, 4, 4, 4, 2), ("zl", "y", "zh", "x", "core"))
    rows = P(DP, CTX, None)
    square = P(DP, CTX)
    return jax.shard_map(
        per_device,
        mesh=fine,
        in_specs=(rows, rows, rows, square, rows, P(DP, None)),
        out_specs=(rows, rows, rows, square),
        check_vma=False,
    )
```

```python
import jax
import jax.numpy as jnp
from jax import lax
from jax.experimental import pallas as pl
from jax.experimental.pallas import tpu as pltpu
from jax.sharding import Mesh
from jax.sharding import PartitionSpec as P

QUERY_HEADS = 32
KV_HEADS = 4
HEAD = 64
WINDOW = 128
KEYF = 256
GROUP = QUERY_HEADS // KV_HEADS
ROWS = 64
rope_base = 150000.0
masked_score = -1e30
bf16 = jnp.bfloat16
f32 = jnp.float32

DP = ("zl", "y")
CTX = ("zh", "x", "core")
Z = ("zl", "zh")
YX = ("y", "x")


def nt(a, b):
    return lax.dot_general(a, b, (((1,), (1,)), ((), ())), preferred_element_type=f32)


def nn(a, b):
    return lax.dot_general(a, b, (((1,), (0,)), ((), ())), preferred_element_type=f32)


def tn(a, b):
    return lax.dot_general(a, b, (((0,), (0,)), ((), ())), preferred_element_type=f32)


def swap_halves(x):
    lane = lax.broadcasted_iota(jnp.int32, x.shape, 1)
    width = x.shape[1]
    return jnp.where(lane % HEAD < HEAD // 2, pltpu.roll(x, width - HEAD // 2, 1), pltpu.roll(x, HEAD // 2, 1))


def pack(tokens_ref, packed_ref):
    parts, _, wide = packed_ref.shape
    width = wide // parts
    for y in range(parts):
        for zl in range(parts):
            at = (zl * parts + y) * width
            packed_ref[y, :, zl * width : (zl + 1) * width] = tokens_ref[:, at : at + width]


def project_kernel(tokens_ref, weight_ref, v_ref, cos_ref, sin_ref, keys_ref, edge_ref, packed_ref):
    parts, rows, _ = packed_ref.shape
    pack(tokens_ref, packed_ref)
    linear = jnp.zeros((rows, KEYF), f32)
    for y in range(parts):
        linear += nt(packed_ref[y], weight_ref[y])
    keys = (linear * cos_ref[...] + swap_halves(linear) * sin_ref[...]).astype(bf16)
    keys_ref[...] = keys
    edge_ref[0] = keys[rows - WINDOW :]
    edge_ref[1] = v_ref[rows - WINDOW :, :]


def band_pairs(q_ref, g_ref, qd_ref, kd_ref, dq_ref, bias_ref, kk_ref, vv_ref, dka_ref, dva_ref, fill):
    blocks = q_ref.shape[0] // ROWS
    span = ROWS + WINDOW
    lanes = GROUP * ROWS

    @pl.when(pl.program_id(0) == 0)
    def _():
        key_at = lax.broadcasted_iota(jnp.int32, (span, lanes), 0)
        query_at = lax.broadcasted_iota(jnp.int32, (span, lanes), 1) % ROWS
        distance = query_at + WINDOW - key_at
        near = (distance >= 0) & (distance <= WINDOW)
        for b in range(blocks):
            same = kd_ref[b * ROWS : b * ROWS + span, :] == qd_ref[b]
            bias_ref[b] = jnp.where(near & same, 0.0, masked_score)

    lane = lax.broadcasted_iota(jnp.int32, (ROWS, 2 * HEAD), 1)
    low = jnp.where(lane < HEAD, 1.0, 0.0).astype(bf16)
    high = jnp.where(lane < HEAD, 0.0, 1.0).astype(bf16)

    def stacked(ref, b, head):
        parts = []
        for p in range(GROUP // 2):
            at = (head * GROUP // 2 + p) * 2 * HEAD
            pair = ref[b * ROWS : (b + 1) * ROWS, at : at + 2 * HEAD]
            parts += [pair * low, pair * high]
        return jnp.concatenate(parts, axis=0)

    for head in range(2):
        fill(head)
        dka_ref[head] = jnp.zeros_like(dka_ref[head])
        dva_ref[head] = jnp.zeros_like(dva_ref[head])
        for b in range(blocks):
            band = slice(b * ROWS, b * ROWS + span)
            keys = kk_ref[band, :]
            values = vv_ref[band, :]
            qs = stacked(q_ref, b, head)
            gs = stacked(g_ref, b, head)
            scores = nt(keys, qs) + bias_ref[b]
            weights = jnp.exp(scores - jnp.max(scores, axis=0, keepdims=True))
            probs = weights * (1.0 / jnp.sum(weights, axis=0, keepdims=True))
            probs_low = probs.astype(bf16)
            prob_grad = nt(values, gs)
            delta = jnp.sum(probs_low.astype(f32) * prob_grad, axis=0, keepdims=True)
            score_low = (probs * (prob_grad - delta)).astype(bf16)
            dva_ref[head, band, :] += nn(probs_low, gs)
            dka_ref[head, band, :] += nn(score_low, qs)
            dq = tn(score_low, keys)
            for p in range(GROUP // 2):
                at = (head * GROUP // 2 + p) * 2 * HEAD
                top = dq[2 * p * ROWS : (2 * p + 1) * ROWS]
                bottom = dq[(2 * p + 1) * ROWS : (2 * p + 2) * ROWS]
                dq_ref[b * ROWS : (b + 1) * ROWS, at : at + 2 * HEAD] = jnp.where(
                    lane < HEAD, top, bottom
                ).astype(bf16)

    def joined(ref):
        first, second = ref[0], ref[1]
        at = lax.broadcasted_iota(jnp.int32, first.shape, 1)
        first = first + pltpu.roll(first, HEAD, 1)
        second = second + pltpu.roll(second, HEAD, 1)
        return jnp.where(at < HEAD, first, second)

    return joined(dka_ref) * 0.125, joined(dva_ref)


def doubled(tile, head, scale):
    wide = tile.astype(f32) * scale
    at = lax.broadcasted_iota(jnp.int32, wide.shape, 1)
    return jnp.where(at // HEAD == head, wide, pltpu.roll(wide, HEAD, 1)).astype(bf16)


def early_kernel(
    q_ref, g_ref, k_ref, v_ref, edge_ref, qd_ref, kd_ref,
    dq_ref, dk_ref, dv_ref, out_edge_ref,
    bias_ref, kk_ref, vv_ref, dka_ref, dva_ref,
):
    def fill(head):
        kk_ref[:WINDOW, :] = doubled(edge_ref[0], head, 0.125)
        kk_ref[WINDOW:, :] = doubled(k_ref[...], head, 0.125)
        vv_ref[:WINDOW, :] = doubled(edge_ref[1], head, 1.0)
        vv_ref[WINDOW:, :] = doubled(v_ref[...], head, 1.0)

    dk, dv = band_pairs(q_ref, g_ref, qd_ref, kd_ref, dq_ref, bias_ref, kk_ref, vv_ref, dka_ref, dva_ref, fill)
    out_edge_ref[0] = dk[:WINDOW].astype(bf16)
    out_edge_ref[1] = dv[:WINDOW].astype(bf16)
    dk_ref[...] = dk[WINDOW:]
    dv_ref[...] = dv[WINDOW:]


def late_kernel(
    q_ref, g_ref, k_ref, v_ref, qd_ref, kd_ref, _,
    dq_ref, dk_ref, dv_ref,
    bias_ref, kk_ref, vv_ref, dka_ref, dva_ref,
):
    def fill(head):
        kk_ref[...] = doubled(k_ref[...], head, 0.125)
        vv_ref[...] = doubled(v_ref[...], head, 1.0)

    dk, dv = band_pairs(q_ref, g_ref, qd_ref, kd_ref, dq_ref, bias_ref, kk_ref, vv_ref, dka_ref, dva_ref, fill)
    dk_ref[...] = dk
    dv_ref[...] = dv


def tail_kernel(
    dk1_ref, dv1_ref, dk2_ref, dv2_ref, edge_ref, cos_ref, sin_ref, tokens_ref, order_ref,
    vg_ref, lin_ref, own_ref, send_ref, packed_ref,
):
    parts, rows, wide = packed_ref.shape
    start = rows - WINDOW

    def total(early_ref, late_ref, edge):
        sums = late_ref[...]
        sums = jnp.concatenate([sums[:WINDOW] + early_ref[...], sums[WINDOW:]], axis=0)
        return jnp.concatenate([sums[:start], sums[start:] + edge.astype(f32)], axis=0)

    vg_ref[...] = total(dv1_ref, dv2_ref, edge_ref[1]).astype(bf16)
    dk = total(dk1_ref, dk2_ref, edge_ref[0])
    lin = (dk * cos_ref[...] - swap_halves(dk) * sin_ref[...]).astype(bf16)
    lin_ref[...] = lin
    ordered = nt(order_ref[...], lin).astype(bf16)
    half = KEYF // 2
    block = (parts, half // parts, wide)
    pack(tokens_ref, packed_ref)
    for y in range(parts):
        to = slice(y * parts, (y + 1) * parts)
        own_ref[to] = nn(ordered[:half], packed_ref[y]).reshape(block)
        send_ref[to] = nn(ordered[half:], packed_ref[y]).reshape(block).astype(bf16)


def input_kernel(lin_ref, weight_ref, ig_ref):
    parts = weight_ref.shape[0]
    width = weight_ref.shape[2] // parts
    for y in range(parts):
        part = nn(lin_ref[...], weight_ref[y]).astype(bf16)
        for zl in range(parts):
            at = (zl * parts + y) * width
            ig_ref[:, at : at + width] = part[:, zl * width : (zl + 1) * width]


def room(mib):
    return pltpu.CompilerParams(vmem_limit_bytes=mib << 20)


def spread(x, axes):
    peers = lax.axis_size(axes)
    return lax.all_to_all(jnp.broadcast_to(x[None], (peers,) + x.shape), axes, 0, 0, tiled=True)


def exchanged(x, axis):
    return lax.ppermute(x, axis, [(0, 1), (1, 0)])


def gathered_weight(block):
    width, sub = block.shape
    zl, y, zh, x = (lax.axis_size(a) for a in ("zl", "y", "zh", "x"))
    along_z = spread(block.T, Z).reshape(zl, zh, sub, width)
    rows = along_z.transpose(1, 2, 0, 3).reshape(zh * sub, zl * width)
    mine = spread(rows, YX)
    other = exchanged(mine, "core")
    first = lax.axis_index("core") == 0
    pair = jnp.stack([jnp.where(first, mine, other), jnp.where(first, other, mine)])
    pair = pair.reshape(2, y, x, zh, sub, zl * width).transpose(1, 3, 2, 0, 4, 5)
    return pair.reshape(y, zh * x * 2 * sub, zl * width)


def summed(x, axes):
    return jnp.sum(lax.all_to_all(x, axes, 0, 0, tiled=True).astype(f32), axis=0)


def scattered_gradient(own, send, beside, width, sub):
    zl, zh = lax.axis_size("zl"), lax.axis_size("zh")
    other, beside = lax.optimization_barrier((exchanged(send, "core"), beside))
    both = (own + other.astype(f32)).astype(bf16)
    over_yx = summed(both, YX).astype(bf16)
    over_yx = over_yx.reshape(zh, sub, zl, width).transpose(2, 0, 1, 3)
    return summed(over_yx.reshape(zl * zh, sub, width), Z), beside


def per_device(tokens_in, queries, values_in, key_weight, out_grad, doc_ids):
    rows = tokens_in.shape[1]
    dim = tokens_in.shape[2]
    width, sub = key_weight.shape
    tokens, q, g, v = tokens_in[0], queries[0], out_grad[0], values_in[0]
    q = pltpu.with_memory_space_constraint(q, pltpu.HBM)
    g = pltpu.with_memory_space_constraint(g, pltpu.HBM)
    blocks = rows // ROWS
    parts = lax.axis_size("y")
    peers = lax.axis_size(CTX)
    position = lax.axis_index(CTX)
    first_row = position * rows

    exponent = jnp.arange(HEAD // 2, dtype=f32) * (-2.0 / HEAD)
    inverse_freq = jnp.power(f32(rope_base), exponent)
    angles = (first_row + jnp.arange(rows, dtype=jnp.int32)).astype(f32)[:, None] * inverse_freq[None, :]
    cosine, sine = jnp.cos(angles), jnp.sin(angles)
    cos_table = jnp.tile(cosine, (1, 2 * KV_HEADS))
    sin_table = jnp.tile(jnp.concatenate([-sine, sine], axis=1), (1, KV_HEADS))

    padded_docs = jnp.concatenate([jnp.full((WINDOW,), -1, jnp.int32), doc_ids[0]])
    band_docs = lax.dynamic_slice_in_dim(padded_docs, first_row, rows + WINDOW)
    query_docs = jnp.tile(band_docs[WINDOW:].reshape(blocks, 1, ROWS), (1, 1, GROUP))
    key_docs = band_docs[:, None]

    core = lax.axis_index("core")
    dest = jnp.arange(KEYF, dtype=jnp.int32)
    rel, dest_x, dest_zh, dest_j = dest // 128, dest // 32 % 4, dest // 8 % 4, dest % 8
    source = dest_zh * 64 + dest_x * 16 + (rel ^ core) * 8 + dest_j
    order = (source[:, None] == jnp.arange(KEYF, dtype=jnp.int32)[None, :]).astype(bf16)

    weight = gathered_weight(key_weight)
    keys, edge = pl.pallas_call(
        project_kernel,
        out_shape=[jax.ShapeDtypeStruct((rows, KEYF), bf16), jax.ShapeDtypeStruct((2, WINDOW, KEYF), bf16)],
        scratch_shapes=[pltpu.VMEM((parts, rows, dim // parts), bf16)],
        compiler_params=room(10),
        name="project",
    )(tokens, weight, v, cos_table, sin_table)

    along = [(i, i + 1) for i in range(peers - 1)]
    back = [(i + 1, i) for i in range(peers - 1)]
    prior = lax.ppermute(edge, CTX, along)

    span = ROWS + WINDOW
    pair = 2 * HEAD
    wide = 2 * GROUP * HEAD
    edge_tile = pl.BlockSpec((2, WINDOW, pair), lambda k: (0, 0, k))

    def tile(size):
        return pl.BlockSpec((size, pair), lambda k: (0, k))

    def heads(size, at):
        return pl.BlockSpec((size, wide), lambda k: (at, k))

    def fixed(shape):
        return pl.BlockSpec(shape, lambda k: (0,) * len(shape))

    def scratch(count):
        band = (count - 1) * ROWS + span
        return [
            pltpu.VMEM((count, span, GROUP * ROWS), f32),
            pltpu.VMEM((band, pair), bf16),
            pltpu.VMEM((band, pair), bf16),
            pltpu.VMEM((2, band, pair), f32),
            pltpu.VMEM((2, band, pair), f32),
        ]

    dq, dk1, dv1, out_edge = pl.pallas_call(
        early_kernel,
        grid=(KV_HEADS // 2,),
        in_specs=[
            heads(WINDOW, 0),
            heads(WINDOW, 0),
            tile(WINDOW),
            tile(WINDOW),
            edge_tile,
            fixed((2, 1, GROUP * ROWS)),
            fixed((2 * WINDOW, 1)),
        ],
        out_specs=[heads(WINDOW, 0), tile(WINDOW), tile(WINDOW), edge_tile],
        out_shape=[
            jax.ShapeDtypeStruct((rows, QUERY_HEADS * HEAD), bf16),
            jax.ShapeDtypeStruct((WINDOW, KEYF), f32),
            jax.ShapeDtypeStruct((WINDOW, KEYF), f32),
            jax.ShapeDtypeStruct((2, WINDOW, KEYF), bf16),
        ],
        scratch_shapes=scratch(2),
        compiler_params=room(16),
        name="band_early",
    )(q, g, keys, v, prior, query_docs[:2], key_docs[: 2 * WINDOW])

    incoming = lax.ppermute(out_edge, CTX, back)

    dq, dk2, dv2 = pl.pallas_call(
        late_kernel,
        grid=(KV_HEADS // 2,),
        in_specs=[
            heads(ROWS, 2),
            heads(ROWS, 2),
            tile(rows),
            tile(rows),
            fixed((1, 1, GROUP * ROWS)),
            fixed((rows, 1)),
            pl.BlockSpec(memory_space=pl.ANY),
        ],
        out_specs=[heads(ROWS, 2), tile(rows), tile(rows)],
        out_shape=[
            jax.ShapeDtypeStruct((rows, QUERY_HEADS * HEAD), bf16),
            jax.ShapeDtypeStruct((rows, KEYF), f32),
            jax.ShapeDtypeStruct((rows, KEYF), f32),
        ],
        input_output_aliases={6: 0},
        scratch_shapes=scratch(1),
        compiler_params=room(16),
        name="band_late",
    )(q, g, keys, v, query_docs[2:], key_docs[WINDOW:], dq)

    value_grad, lin, own, send = pl.pallas_call(
        tail_kernel,
        out_shape=[
            jax.ShapeDtypeStruct((rows, KEYF), bf16),
            jax.ShapeDtypeStruct((rows, KEYF), bf16),
            jax.ShapeDtypeStruct((parts * parts, KEYF // 2 // parts, dim // parts), f32),
            jax.ShapeDtypeStruct((parts * parts, KEYF // 2 // parts, dim // parts), bf16),
        ],
        scratch_shapes=[pltpu.VMEM((parts, rows, dim // parts), bf16)],
        compiler_params=room(16),
        name="tail",
    )(dk1, dv1, dk2, dv2, incoming, cos_table, sin_table, tokens, order)
    input_grad = pl.pallas_call(
        input_kernel,
        out_shape=jax.ShapeDtypeStruct((rows, dim), bf16),
        compiler_params=room(8),
        name="input_grad",
    )(lin, weight)

    weight_grad, input_grad = scattered_gradient(own, send, input_grad, width, sub)
    return dq[None], value_grad[None], input_grad[None], weight_grad.T


def solution(mesh):
    fine = Mesh(mesh.devices.reshape(4, 4, 4, 4, 2), ("zl", "y", "zh", "x", "core"))
    rows = P(DP, CTX, None)
    square = P(DP, CTX)
    return jax.shard_map(
        per_device,
        mesh=fine,
        in_specs=(rows, rows, rows, square, rows, P(DP, None)),
        out_specs=(rows, rows, rows, square),
        check_vma=False,
    )
```

```python
import jax
import jax.numpy as jnp
from jax import lax
from jax.experimental import pallas as pl
from jax.experimental.pallas import tpu as pltpu
from jax.sharding import Mesh
from jax.sharding import PartitionSpec as P

QUERY_HEADS = 32
KV_HEADS = 4
HEAD = 64
WINDOW = 128
KEYF = 256
GROUP = QUERY_HEADS // KV_HEADS
ROWS = 64
rope_base = 150000.0
masked_score = -1e30
bf16 = jnp.bfloat16
f32 = jnp.float32

DP = ("zl", "y")
CTX = ("zh", "x", "core")
Z = ("zl", "zh")
YX = ("y", "x")


def nt(a, b):
    return lax.dot_general(a, b, (((1,), (1,)), ((), ())), preferred_element_type=f32)


def nn(a, b):
    return lax.dot_general(a, b, (((1,), (0,)), ((), ())), preferred_element_type=f32)


def tn(a, b):
    return lax.dot_general(a, b, (((0,), (0,)), ((), ())), preferred_element_type=f32)


def swap_halves(x):
    lane = lax.broadcasted_iota(jnp.int32, x.shape, 1)
    width = x.shape[1]
    return jnp.where(lane % HEAD < HEAD // 2, pltpu.roll(x, width - HEAD // 2, 1), pltpu.roll(x, HEAD // 2, 1))


def pack(tokens_ref, packed_ref):
    parts, _, wide = packed_ref.shape
    width = wide // parts
    for y in range(parts):
        for zl in range(parts):
            at = (zl * parts + y) * width
            packed_ref[y, :, zl * width : (zl + 1) * width] = tokens_ref[:, at : at + width]


def half_linear(packed_ref, half_ref):
    parts, rows, wide = packed_ref.shape
    total = jnp.zeros((rows, KEYF // 2), f32)
    for y in range(parts):
        total += nt(packed_ref[y], half_ref[y * parts : (y + 1) * parts].reshape(KEYF // 2, wide))
    return total


def first_kernel(tokens_ref, mine_ref, packed_ref, linear_ref):
    pack(tokens_ref, packed_ref)
    linear_ref[...] = half_linear(packed_ref, mine_ref)


def table(ref):
    return jnp.concatenate([ref[...], ref[...]], axis=1)


def project_kernel(packed_ref, other_ref, linear_ref, order_ref, v_ref, cos_ref, sin_ref, keys_ref, edge_ref):
    rows = packed_ref.shape[1]
    gathered = jnp.concatenate([linear_ref[...], half_linear(packed_ref, other_ref)], axis=1)
    top = gathered.astype(bf16)
    rest = gathered - top.astype(f32)
    middle = rest.astype(bf16)
    bottom = (rest - middle.astype(f32)).astype(bf16)
    order = order_ref[...]
    linear = nn(top, order) + (nn(middle, order) + nn(bottom, order))
    keys = (linear * table(cos_ref) + swap_halves(linear) * table(sin_ref)).astype(bf16)
    keys_ref[...] = keys
    edge_ref[0] = keys[rows - WINDOW :]
    edge_ref[1] = v_ref[rows - WINDOW :, :]


def band_pairs(q_ref, g_ref, low_ref, dq_ref, bias_ref, kk_ref, vv_ref, dka_ref, dva_ref, fill):
    blocks = q_ref.shape[0] // ROWS
    span = ROWS + WINDOW
    lanes = GROUP * ROWS

    @pl.when(pl.program_id(0) == 0)
    def _():
        key_at = lax.broadcasted_iota(jnp.int32, (span, lanes), 0)
        last = lax.broadcasted_iota(jnp.int32, (1, lanes), 1) % ROWS + WINDOW
        for b in range(blocks):
            bias_ref[b] = jnp.where((key_at >= low_ref[b]) & (key_at <= last), 0.0, masked_score)

    lane = lax.broadcasted_iota(jnp.int32, (ROWS, 2 * HEAD), 1)
    low = jnp.where(lane < HEAD, 1.0, 0.0).astype(bf16)
    high = jnp.where(lane < HEAD, 0.0, 1.0).astype(bf16)

    def stacked(ref, b, head):
        parts = []
        for p in range(GROUP // 2):
            at = (head * GROUP // 2 + p) * 2 * HEAD
            pair = ref[b * ROWS : (b + 1) * ROWS, at : at + 2 * HEAD]
            parts += [pair * low, pair * high]
        return jnp.concatenate(parts, axis=0)

    for head in range(2):
        fill(head)
        dka_ref[head] = jnp.zeros_like(dka_ref[head])
        dva_ref[head] = jnp.zeros_like(dva_ref[head])
        for b in range(blocks):
            band = slice(b * ROWS, b * ROWS + span)
            keys = kk_ref[band, :]
            values = vv_ref[band, :]
            qs = stacked(q_ref, b, head)
            gs = stacked(g_ref, b, head)
            scores = nt(keys, qs) + bias_ref[b]
            weights = jnp.exp(scores - jnp.max(scores, axis=0, keepdims=True))
            probs = weights * (1.0 / jnp.sum(weights, axis=0, keepdims=True))
            probs_low = probs.astype(bf16)
            prob_grad = nt(values, gs)
            delta = jnp.sum(probs_low.astype(f32) * prob_grad, axis=0, keepdims=True)
            score_low = (probs * (prob_grad - delta)).astype(bf16)
            dva_ref[head, band, :] += nn(probs_low, gs)
            dka_ref[head, band, :] += nn(score_low, qs)
            dq = tn(score_low, keys)
            for p in range(GROUP // 2):
                at = (head * GROUP // 2 + p) * 2 * HEAD
                top = dq[2 * p * ROWS : (2 * p + 1) * ROWS]
                bottom = dq[(2 * p + 1) * ROWS : (2 * p + 2) * ROWS]
                dq_ref[b * ROWS : (b + 1) * ROWS, at : at + 2 * HEAD] = jnp.where(
                    lane < HEAD, top, bottom
                ).astype(bf16)

    def joined(ref):
        first, second = ref[0], ref[1]
        at = lax.broadcasted_iota(jnp.int32, first.shape, 1)
        first = first + pltpu.roll(first, HEAD, 1)
        second = second + pltpu.roll(second, HEAD, 1)
        return jnp.where(at < HEAD, first, second)

    return joined(dka_ref) * 0.125, joined(dva_ref)


def doubled(tile, head, scale):
    wide = tile.astype(f32) * scale
    at = lax.broadcasted_iota(jnp.int32, wide.shape, 1)
    return jnp.where(at // HEAD == head, wide, pltpu.roll(wide, HEAD, 1)).astype(bf16)


def early_kernel(
    q_ref, g_ref, k_ref, v_ref, edge_ref, low_ref,
    dq_ref, dk_ref, dv_ref, out_edge_ref,
    bias_ref, kk_ref, vv_ref, dka_ref, dva_ref,
):
    def fill(head):
        kk_ref[:WINDOW, :] = doubled(edge_ref[0], head, 0.125)
        kk_ref[WINDOW:, :] = doubled(k_ref[...], head, 0.125)
        vv_ref[:WINDOW, :] = doubled(edge_ref[1], head, 1.0)
        vv_ref[WINDOW:, :] = doubled(v_ref[...], head, 1.0)

    dk, dv = band_pairs(q_ref, g_ref, low_ref, dq_ref, bias_ref, kk_ref, vv_ref, dka_ref, dva_ref, fill)
    out_edge_ref[0] = dk[:WINDOW].astype(bf16)
    out_edge_ref[1] = dv[:WINDOW].astype(bf16)
    dk_ref[...] = dk[WINDOW:]
    dv_ref[...] = dv[WINDOW:]


def late_kernel(
    q_ref, g_ref, k_ref, v_ref, low_ref, _,
    dq_ref, dk_ref, dv_ref,
    bias_ref, kk_ref, vv_ref, dka_ref, dva_ref,
):
    def fill(head):
        kk_ref[...] = doubled(k_ref[...], head, 0.125)
        vv_ref[...] = doubled(v_ref[...], head, 1.0)

    dk, dv = band_pairs(q_ref, g_ref, low_ref, dq_ref, bias_ref, kk_ref, vv_ref, dka_ref, dva_ref, fill)
    dk_ref[...] = dk
    dv_ref[...] = dv


def tail_kernel(
    dk1_ref, dv1_ref, dk2_ref, dv2_ref, edge_ref, cos_ref, sin_ref, tokens_ref, order_ref,
    vg_ref, lin_ref, own_ref, send_ref, packed_ref,
):
    parts, rows, wide = packed_ref.shape
    start = rows - WINDOW

    def total(early_ref, late_ref, edge):
        sums = late_ref[...]
        sums = jnp.concatenate([sums[:WINDOW] + early_ref[...], sums[WINDOW:]], axis=0)
        return jnp.concatenate([sums[:start], sums[start:] + edge.astype(f32)], axis=0)

    vg_ref[...] = total(dv1_ref, dv2_ref, edge_ref[1]).astype(bf16)
    dk = total(dk1_ref, dk2_ref, edge_ref[0])
    lin = (dk * table(cos_ref) - swap_halves(dk) * table(sin_ref)).astype(bf16)
    lin_ref[...] = lin
    ordered = nt(order_ref[...], lin).astype(bf16)
    half = KEYF // 2
    block = (parts, half // parts, wide)
    pack(tokens_ref, packed_ref)
    for y in range(parts):
        to = slice(y * parts, (y + 1) * parts)
        own_ref[to] = nn(ordered[:half], packed_ref[y]).reshape(block)
        send_ref[to] = nn(ordered[half:], packed_ref[y]).reshape(block).astype(bf16)


def input_kernel(lin_ref, order_ref, mine_ref, other_ref, ig_ref):
    parts = 4
    wide = mine_ref.shape[2]
    width = wide // parts
    half = KEYF // 2
    ordered = nt(lin_ref[...], order_ref[...]).astype(bf16)
    for y in range(parts):
        at = slice(y * parts, (y + 1) * parts)
        part = nn(ordered[:, :half], mine_ref[at].reshape(half, wide))
        part = (part + nn(ordered[:, half:], other_ref[at].reshape(half, wide))).astype(bf16)
        for zl in range(parts):
            at = (zl * parts + y) * width
            ig_ref[:, at : at + width] = part[:, zl * width : (zl + 1) * width]


def room(mib):
    return pltpu.CompilerParams(vmem_limit_bytes=mib << 20)


def spread(x, axes):
    peers = lax.axis_size(axes)
    return lax.all_to_all(jnp.broadcast_to(x[None], (peers,) + x.shape), axes, 0, 0, tiled=True)


def exchanged(x, axis):
    return lax.ppermute(x, axis, [(0, 1), (1, 0)])


def gathered_weight(block):
    width, sub = block.shape
    zl, zh = lax.axis_size("zl"), lax.axis_size("zh")
    along_z = spread(block.T, Z).reshape(zl, zh, sub, width)
    return spread(along_z.transpose(1, 2, 0, 3).reshape(zh * sub, zl * width), YX)


def summed(x, axes):
    return jnp.sum(lax.all_to_all(x, axes, 0, 0, tiled=True).astype(f32), axis=0)


def scattered_gradient(own, send, beside, width, sub):
    zl, zh = lax.axis_size("zl"), lax.axis_size("zh")
    other, beside = lax.optimization_barrier((exchanged(send, "core"), beside))
    both = (own + other.astype(f32)).astype(bf16)
    over_yx = summed(both, YX).astype(bf16)
    over_yx = over_yx.reshape(zh, sub, zl, width).transpose(2, 0, 1, 3)
    return summed(over_yx.reshape(zl * zh, sub, width), Z), beside


def per_device(tokens_in, queries, values_in, key_weight, out_grad, doc_ids):
    rows = tokens_in.shape[1]
    dim = tokens_in.shape[2]
    width, sub = key_weight.shape
    tokens, q, g, v = tokens_in[0], queries[0], out_grad[0], values_in[0]
    q = pltpu.with_memory_space_constraint(q, pltpu.HBM)
    g = pltpu.with_memory_space_constraint(g, pltpu.HBM)
    blocks = rows // ROWS
    parts = lax.axis_size("y")
    peers = lax.axis_size(CTX)
    mine = gathered_weight(key_weight)
    mine, position, core, docs = lax.optimization_barrier(
        (mine, lax.axis_index(CTX), lax.axis_index("core"), doc_ids[0])
    )
    first_row = position * rows

    lane = jnp.arange(2 * HEAD, dtype=jnp.int32)
    exponent = (lane % (HEAD // 2)).astype(f32) * (-2.0 / HEAD)
    inverse_freq = jnp.power(f32(rope_base), exponent)
    angles = (first_row + jnp.arange(rows, dtype=jnp.int32)).astype(f32)[:, None] * inverse_freq[None, :]
    cos_table = jnp.cos(angles)
    sin_table = jnp.sin(angles) * jnp.where(lane % HEAD < HEAD // 2, -1.0, 1.0)[None, :]

    padded_docs = jnp.concatenate([jnp.full((WINDOW,), -1, jnp.int32), docs])
    band_docs = lax.dynamic_slice_in_dim(padded_docs, first_row, rows + WINDOW)
    lowest = jnp.sum((band_docs[:, None] < band_docs[None, WINDOW:]).astype(jnp.int32), axis=0)
    block_row = jnp.arange(rows, dtype=jnp.int32)
    lowest = jnp.maximum(lowest - block_row // ROWS * ROWS, block_row % ROWS)
    lowest = jnp.tile(lowest.reshape(blocks, 1, ROWS), (1, 1, GROUP))

    dest = jnp.arange(KEYF, dtype=jnp.int32)
    rel, dest_x, dest_zh, dest_j = dest // 128, dest // 32 % 4, dest // 8 % 4, dest % 8
    source = dest_zh * 64 + dest_x * 16 + (rel ^ core) * 8 + dest_j
    order = (source[:, None] == jnp.arange(KEYF, dtype=jnp.int32)[None, :]).astype(bf16)

    other = exchanged(mine, "core")
    packed, linear = pl.pallas_call(
        first_kernel,
        out_shape=[
            jax.ShapeDtypeStruct((parts, rows, dim // parts), bf16),
            jax.ShapeDtypeStruct((rows, KEYF // 2), f32),
        ],
        compiler_params=room(16),
        name="project_own",
    )(tokens, mine)
    keys, edge = pl.pallas_call(
        project_kernel,
        out_shape=[jax.ShapeDtypeStruct((rows, KEYF), bf16), jax.ShapeDtypeStruct((2, WINDOW, KEYF), bf16)],
        compiler_params=room(16),
        name="project",
    )(packed, other, linear, order, v, cos_table, sin_table)

    along = [(i, i + 1) for i in range(peers - 1)]
    back = [(i + 1, i) for i in range(peers - 1)]
    prior = lax.ppermute(edge, CTX, along)

    span = ROWS + WINDOW
    pair = 2 * HEAD
    wide = 2 * GROUP * HEAD
    edge_tile = pl.BlockSpec((2, WINDOW, pair), lambda k: (0, 0, k))

    def tile(size):
        return pl.BlockSpec((size, pair), lambda k: (0, k))

    def heads(size, at):
        return pl.BlockSpec((size, wide), lambda k: (at, k))

    def scratch(count):
        band = (count - 1) * ROWS + span
        return [
            pltpu.VMEM((count, span, GROUP * ROWS), f32),
            pltpu.VMEM((band, pair), bf16),
            pltpu.VMEM((band, pair), bf16),
            pltpu.VMEM((2, band, pair), f32),
            pltpu.VMEM((2, band, pair), f32),
        ]

    dq, dk1, dv1, out_edge = pl.pallas_call(
        early_kernel,
        grid=(KV_HEADS // 2,),
        in_specs=[
            heads(WINDOW, 0),
            heads(WINDOW, 0),
            tile(WINDOW),
            tile(WINDOW),
            edge_tile,
            pl.BlockSpec((2, 1, GROUP * ROWS), lambda k: (0, 0, 0)),
        ],
        out_specs=[heads(WINDOW, 0), tile(WINDOW), tile(WINDOW), edge_tile],
        out_shape=[
            jax.ShapeDtypeStruct((rows, QUERY_HEADS * HEAD), bf16),
            jax.ShapeDtypeStruct((WINDOW, KEYF), f32),
            jax.ShapeDtypeStruct((WINDOW, KEYF), f32),
            jax.ShapeDtypeStruct((2, WINDOW, KEYF), bf16),
        ],
        scratch_shapes=scratch(2),
        compiler_params=room(16),
        name="band_early",
    )(q, g, keys, v, prior, lowest)

    incoming = lax.ppermute(out_edge, CTX, back)

    dq, dk2, dv2 = pl.pallas_call(
        late_kernel,
        grid=(KV_HEADS // 2,),
        in_specs=[
            heads(ROWS, 2),
            heads(ROWS, 2),
            tile(rows),
            tile(rows),
            pl.BlockSpec((1, 1, GROUP * ROWS), lambda k: (2, 0, 0)),
            pl.BlockSpec(memory_space=pl.ANY),
        ],
        out_specs=[heads(ROWS, 2), tile(rows), tile(rows)],
        out_shape=[
            jax.ShapeDtypeStruct((rows, QUERY_HEADS * HEAD), bf16),
            jax.ShapeDtypeStruct((rows, KEYF), f32),
            jax.ShapeDtypeStruct((rows, KEYF), f32),
        ],
        input_output_aliases={5: 0},
        scratch_shapes=scratch(1),
        compiler_params=room(16),
        name="band_late",
    )(q, g, keys, v, lowest, dq)

    value_grad, lin, own, send = pl.pallas_call(
        tail_kernel,
        out_shape=[
            jax.ShapeDtypeStruct((rows, KEYF), bf16),
            jax.ShapeDtypeStruct((rows, KEYF), bf16),
            jax.ShapeDtypeStruct((parts * parts, KEYF // 2 // parts, dim // parts), f32),
            jax.ShapeDtypeStruct((parts * parts, KEYF // 2 // parts, dim // parts), bf16),
        ],
        scratch_shapes=[pltpu.VMEM((parts, rows, dim // parts), bf16)],
        compiler_params=room(16),
        name="tail",
    )(dk1, dv1, dk2, dv2, incoming, cos_table, sin_table, tokens, order)
    input_grad = pl.pallas_call(
        input_kernel,
        out_shape=jax.ShapeDtypeStruct((rows, dim), bf16),
        compiler_params=room(8),
        name="input_grad",
    )(lin, order, mine, other)

    weight_grad, input_grad = scattered_gradient(own, send, input_grad, width, sub)
    return dq[None], value_grad[None], input_grad[None], weight_grad.T


def solution(mesh):
    fine = Mesh(mesh.devices.reshape(4, 4, 4, 4, 2), ("zl", "y", "zh", "x", "core"))
    rows = P(DP, CTX, None)
    square = P(DP, CTX)
    return jax.shard_map(
        per_device,
        mesh=fine,
        in_specs=(rows, rows, rows, square, rows, P(DP, None)),
        out_specs=(rows, rows, rows, square),
        check_vma=False,
    )
```

```python
import jax
import jax.numpy as jnp
from jax import lax
from jax.experimental import pallas as pl
from jax.experimental.pallas import tpu as pltpu
from jax.sharding import Mesh
from jax.sharding import PartitionSpec as P

QUERY_HEADS = 32
KV_HEADS = 4
HEAD = 64
WINDOW = 128
KEYF = 256
GROUP = QUERY_HEADS // KV_HEADS
ROWS = 64
rope_base = 150000.0
masked_score = -1e30
bf16 = jnp.bfloat16
f32 = jnp.float32

DP = ("zl", "y")
CTX = ("zh", "x", "core")
Z = ("zl", "zh")
YX = ("y", "x")


def nt(a, b):
    return lax.dot_general(a, b, (((1,), (1,)), ((), ())), preferred_element_type=f32)


def nn(a, b):
    return lax.dot_general(a, b, (((1,), (0,)), ((), ())), preferred_element_type=f32)


def tn(a, b):
    return lax.dot_general(a, b, (((0,), (0,)), ((), ())), preferred_element_type=f32)


def swap_halves(x):
    lane = lax.broadcasted_iota(jnp.int32, x.shape, 1)
    width = x.shape[1]
    return jnp.where(lane % HEAD < HEAD // 2, pltpu.roll(x, width - HEAD // 2, 1), pltpu.roll(x, HEAD // 2, 1))


def pack(tokens_ref, packed_ref):
    parts, _, wide = packed_ref.shape
    width = wide // parts
    for y in range(parts):
        for zl in range(parts):
            at = (zl * parts + y) * width
            packed_ref[y, :, zl * width : (zl + 1) * width] = tokens_ref[:, at : at + width]


def half_linear(packed_ref, half_ref):
    parts, rows, wide = packed_ref.shape
    total = jnp.zeros((rows, KEYF // 2), f32)
    for y in range(parts):
        total += nt(packed_ref[y], half_ref[y * parts : (y + 1) * parts].reshape(KEYF // 2, wide))
    return total


def first_kernel(tokens_ref, mine_ref, packed_ref, linear_ref):
    pack(tokens_ref, packed_ref)
    linear_ref[...] = half_linear(packed_ref, mine_ref)


def table(ref):
    return jnp.concatenate([ref[...], ref[...]], axis=1)


def project_kernel(packed_ref, other_ref, linear_ref, order_ref, cos_ref, sin_ref, keys_ref, edge_ref):
    rows = packed_ref.shape[1]
    gathered = jnp.concatenate([linear_ref[...], half_linear(packed_ref, other_ref)], axis=1)
    top = gathered.astype(bf16)
    rest = gathered - top.astype(f32)
    middle = rest.astype(bf16)
    bottom = (rest - middle.astype(f32)).astype(bf16)
    order = order_ref[...]
    linear = nn(top, order) + (nn(middle, order) + nn(bottom, order))
    keys = (linear * table(cos_ref) + swap_halves(linear) * table(sin_ref)).astype(bf16)
    keys_ref[...] = keys
    edge_ref[...] = keys[rows - WINDOW :]


def band_pairs(q_ref, g_ref, low_ref, dq_ref, bias_ref, kk_ref, vv_ref, dka_ref, dva_ref, fill):
    blocks = q_ref.shape[0] // ROWS
    span = ROWS + WINDOW
    lanes = GROUP * ROWS

    @pl.when(pl.program_id(0) == 0)
    def _():
        key_at = lax.broadcasted_iota(jnp.int32, (span, lanes), 0)
        last = lax.broadcasted_iota(jnp.int32, (1, lanes), 1) % ROWS + WINDOW
        for b in range(blocks):
            bias_ref[b] = jnp.where((key_at >= low_ref[b]) & (key_at <= last), 0.0, masked_score)

    lane = lax.broadcasted_iota(jnp.int32, (ROWS, 2 * HEAD), 1)
    low = jnp.where(lane < HEAD, 1.0, 0.0).astype(bf16)
    high = jnp.where(lane < HEAD, 0.0, 1.0).astype(bf16)

    def stacked(ref, b, head):
        parts = []
        for p in range(GROUP // 2):
            at = (head * GROUP // 2 + p) * 2 * HEAD
            pair = ref[b * ROWS : (b + 1) * ROWS, at : at + 2 * HEAD]
            parts += [pair * low, pair * high]
        return jnp.concatenate(parts, axis=0)

    for head in range(2):
        fill(head)
        dka_ref[head] = jnp.zeros_like(dka_ref[head])
        dva_ref[head] = jnp.zeros_like(dva_ref[head])
        for b in range(blocks):
            band = slice(b * ROWS, b * ROWS + span)
            keys = kk_ref[band, :]
            values = vv_ref[band, :]
            qs = stacked(q_ref, b, head)
            gs = stacked(g_ref, b, head)
            scores = nt(keys, qs) + bias_ref[b]
            weights = jnp.exp(scores - jnp.max(scores, axis=0, keepdims=True))
            probs = weights * (1.0 / jnp.sum(weights, axis=0, keepdims=True))
            probs_low = probs.astype(bf16)
            prob_grad = nt(values, gs)
            delta = jnp.sum(probs_low.astype(f32) * prob_grad, axis=0, keepdims=True)
            score_low = (probs * (prob_grad - delta)).astype(bf16)
            dva_ref[head, band, :] += nn(probs_low, gs)
            dka_ref[head, band, :] += nn(score_low, qs)
            dq = tn(score_low, keys)
            for p in range(GROUP // 2):
                at = (head * GROUP // 2 + p) * 2 * HEAD
                top = dq[2 * p * ROWS : (2 * p + 1) * ROWS]
                bottom = dq[(2 * p + 1) * ROWS : (2 * p + 2) * ROWS]
                dq_ref[b * ROWS : (b + 1) * ROWS, at : at + 2 * HEAD] = jnp.where(
                    lane < HEAD, top, bottom
                ).astype(bf16)

    def joined(ref):
        first, second = ref[0], ref[1]
        at = lax.broadcasted_iota(jnp.int32, first.shape, 1)
        first = first + pltpu.roll(first, HEAD, 1)
        second = second + pltpu.roll(second, HEAD, 1)
        return jnp.where(at < HEAD, first, second)

    return joined(dka_ref) * 0.125, joined(dva_ref)


def doubled(tile, head, scale):
    wide = tile.astype(f32) * scale
    at = lax.broadcasted_iota(jnp.int32, wide.shape, 1)
    return jnp.where(at // HEAD == head, wide, pltpu.roll(wide, HEAD, 1)).astype(bf16)


def early_kernel(
    q_ref, g_ref, k_ref, v_ref, prior_k_ref, prior_v_ref, low_ref,
    dq_ref, dk_ref, dv_ref, out_edge_ref,
    bias_ref, kk_ref, vv_ref, dka_ref, dva_ref,
):
    def fill(head):
        kk_ref[:WINDOW, :] = doubled(prior_k_ref[...], head, 0.125)
        kk_ref[WINDOW:, :] = doubled(k_ref[...], head, 0.125)
        vv_ref[:WINDOW, :] = doubled(prior_v_ref[...], head, 1.0)
        vv_ref[WINDOW:, :] = doubled(v_ref[...], head, 1.0)

    dk, dv = band_pairs(q_ref, g_ref, low_ref, dq_ref, bias_ref, kk_ref, vv_ref, dka_ref, dva_ref, fill)
    out_edge_ref[0] = dk[:WINDOW].astype(bf16)
    out_edge_ref[1] = dv[:WINDOW].astype(bf16)
    dk_ref[...] = dk[WINDOW:]
    dv_ref[...] = dv[WINDOW:]


def late_kernel(
    q_ref, g_ref, k_ref, v_ref, low_ref, _,
    dq_ref, dk_ref, dv_ref,
    bias_ref, kk_ref, vv_ref, dka_ref, dva_ref,
):
    def fill(head):
        kk_ref[...] = doubled(k_ref[...], head, 0.125)
        vv_ref[...] = doubled(v_ref[...], head, 1.0)

    dk, dv = band_pairs(q_ref, g_ref, low_ref, dq_ref, bias_ref, kk_ref, vv_ref, dka_ref, dva_ref, fill)
    dk_ref[...] = dk
    dv_ref[...] = dv


def total(early_ref, late_ref, edge):
    sums = late_ref[...]
    start = sums.shape[0] - WINDOW
    sums = jnp.concatenate([sums[:WINDOW] + early_ref[...], sums[WINDOW:]], axis=0)
    return jnp.concatenate([sums[:start], sums[start:] + edge.astype(f32)], axis=0)


def tail_kernel(
    early_ref, late_ref, edge_ref, cos_ref, sin_ref, tokens_ref, order_ref,
    lin_ref, own_ref, send_ref, packed_ref,
):
    parts, rows, wide = packed_ref.shape
    dk = total(early_ref, late_ref, edge_ref[0])
    lin = (dk * table(cos_ref) - swap_halves(dk) * table(sin_ref)).astype(bf16)
    lin_ref[...] = lin
    ordered = nt(order_ref[...], lin).astype(bf16)
    half = KEYF // 2
    block = (parts, half // parts, wide)
    pack(tokens_ref, packed_ref)
    for y in range(parts):
        to = slice(y * parts, (y + 1) * parts)
        own_ref[to] = nn(ordered[:half], packed_ref[y]).reshape(block)
        send_ref[to] = nn(ordered[half:], packed_ref[y]).reshape(block).astype(bf16)


def input_kernel(lin_ref, order_ref, mine_ref, other_ref, early_ref, late_ref, edge_ref, ig_ref, vg_ref):
    vg_ref[...] = total(early_ref, late_ref, edge_ref[1]).astype(bf16)
    parts = 4
    wide = mine_ref.shape[2]
    width = wide // parts
    half = KEYF // 2
    ordered = nt(lin_ref[...], order_ref[...]).astype(bf16)
    for y in range(parts):
        at = slice(y * parts, (y + 1) * parts)
        part = nn(ordered[:, :half], mine_ref[at].reshape(half, wide))
        part = (part + nn(ordered[:, half:], other_ref[at].reshape(half, wide))).astype(bf16)
        for zl in range(parts):
            at = (zl * parts + y) * width
            ig_ref[:, at : at + width] = part[:, zl * width : (zl + 1) * width]


def room(mib):
    return pltpu.CompilerParams(vmem_limit_bytes=mib << 20)


def spread(x, axes):
    peers = lax.axis_size(axes)
    return lax.all_to_all(jnp.broadcast_to(x[None], (peers,) + x.shape), axes, 0, 0, tiled=True)


def exchanged(x, axis):
    return lax.ppermute(x, axis, [(0, 1), (1, 0)])


def gathered_weight(block):
    width, sub = block.shape
    zl, zh = lax.axis_size("zl"), lax.axis_size("zh")
    along_z = spread(block.T, Z).reshape(zl, zh, sub, width)
    return spread(along_z.transpose(1, 2, 0, 3).reshape(zh * sub, zl * width), YX)


def summed(x, axes):
    return jnp.sum(lax.all_to_all(x, axes, 0, 0, tiled=True).astype(f32), axis=0)


def scattered_gradient(own, send, beside, width, sub):
    zl, zh = lax.axis_size("zl"), lax.axis_size("zh")
    other, beside = lax.optimization_barrier((exchanged(send, "core"), beside))
    both = (own + other.astype(f32)).astype(bf16)
    over_yx = summed(both, YX).astype(bf16)
    over_yx = over_yx.reshape(zh, sub, zl, width).transpose(2, 0, 1, 3)
    return summed(over_yx.reshape(zl * zh, sub, width), Z), beside


def per_device(tokens_in, queries, values_in, key_weight, out_grad, doc_ids):
    rows = tokens_in.shape[1]
    dim = tokens_in.shape[2]
    width, sub = key_weight.shape
    tokens, q, g, v = tokens_in[0], queries[0], out_grad[0], values_in[0]
    q = pltpu.with_memory_space_constraint(q, pltpu.HBM)
    g = pltpu.with_memory_space_constraint(g, pltpu.HBM)
    blocks = rows // ROWS
    parts = lax.axis_size("y")
    peers = lax.axis_size(CTX)
    along = [(i, i + 1) for i in range(peers - 1)]
    back = [(i + 1, i) for i in range(peers - 1)]
    prior_v = lax.ppermute(v[rows - WINDOW :], CTX, along)

    mine = gathered_weight(key_weight)
    mine, position, core, docs = lax.optimization_barrier(
        (mine, lax.axis_index(CTX), lax.axis_index("core"), doc_ids[0])
    )
    first_row = position * rows

    lane = jnp.arange(2 * HEAD, dtype=jnp.int32)
    exponent = (lane % (HEAD // 2)).astype(f32) * (-2.0 / HEAD)
    inverse_freq = jnp.power(f32(rope_base), exponent)
    angles = (first_row + jnp.arange(rows, dtype=jnp.int32)).astype(f32)[:, None] * inverse_freq[None, :]
    cos_table = jnp.cos(angles)
    sin_table = jnp.sin(angles) * jnp.where(lane % HEAD < HEAD // 2, -1.0, 1.0)[None, :]

    padded_docs = jnp.concatenate([jnp.full((WINDOW,), -1, jnp.int32), docs])
    band_docs = lax.dynamic_slice_in_dim(padded_docs, first_row, rows + WINDOW)
    lowest = jnp.sum((band_docs[:, None] < band_docs[None, WINDOW:]).astype(jnp.int32), axis=0)
    block_row = jnp.arange(rows, dtype=jnp.int32)
    lowest = jnp.maximum(lowest - block_row // ROWS * ROWS, block_row % ROWS)
    lowest = jnp.tile(lowest.reshape(blocks, 1, ROWS), (1, 1, GROUP))

    dest = jnp.arange(KEYF, dtype=jnp.int32)
    rel, dest_x, dest_zh, dest_j = dest // 128, dest // 32 % 4, dest // 8 % 4, dest % 8
    source = dest_zh * 64 + dest_x * 16 + (rel ^ core) * 8 + dest_j
    order = (source[:, None] == jnp.arange(KEYF, dtype=jnp.int32)[None, :]).astype(bf16)

    other = exchanged(mine, "core")
    packed, linear = pl.pallas_call(
        first_kernel,
        out_shape=[
            jax.ShapeDtypeStruct((parts, rows, dim // parts), bf16),
            jax.ShapeDtypeStruct((rows, KEYF // 2), f32),
        ],
        compiler_params=room(16),
        name="project_own",
    )(tokens, mine)
    keys, edge = pl.pallas_call(
        project_kernel,
        out_shape=[jax.ShapeDtypeStruct((rows, KEYF), bf16), jax.ShapeDtypeStruct((WINDOW, KEYF), bf16)],
        compiler_params=room(16),
        name="project",
    )(packed, other, linear, order, cos_table, sin_table)

    prior_k = lax.ppermute(edge, CTX, along)

    span = ROWS + WINDOW
    pair = 2 * HEAD
    wide = 2 * GROUP * HEAD

    def tile(size):
        return pl.BlockSpec((size, pair), lambda k: (0, k))

    def heads(size, at):
        return pl.BlockSpec((size, wide), lambda k: (at, k))

    def scratch(count):
        band = (count - 1) * ROWS + span
        return [
            pltpu.VMEM((count, span, GROUP * ROWS), f32),
            pltpu.VMEM((band, pair), bf16),
            pltpu.VMEM((band, pair), bf16),
            pltpu.VMEM((2, band, pair), f32),
            pltpu.VMEM((2, band, pair), f32),
        ]

    dq, dk1, dv1, out_edge = pl.pallas_call(
        early_kernel,
        grid=(KV_HEADS // 2,),
        in_specs=[
            heads(WINDOW, 0),
            heads(WINDOW, 0),
            tile(WINDOW),
            tile(WINDOW),
            tile(WINDOW),
            tile(WINDOW),
            pl.BlockSpec((2, 1, GROUP * ROWS), lambda k: (0, 0, 0)),
        ],
        out_specs=[heads(WINDOW, 0), tile(WINDOW), tile(WINDOW), pl.BlockSpec((2, WINDOW, pair), lambda k: (0, 0, k))],
        out_shape=[
            jax.ShapeDtypeStruct((rows, QUERY_HEADS * HEAD), bf16),
            jax.ShapeDtypeStruct((WINDOW, KEYF), f32),
            jax.ShapeDtypeStruct((WINDOW, KEYF), f32),
            jax.ShapeDtypeStruct((2, WINDOW, KEYF), bf16),
        ],
        scratch_shapes=scratch(2),
        compiler_params=room(16),
        name="band_early",
    )(q, g, keys, v, prior_k, prior_v, lowest)

    incoming = lax.ppermute(out_edge, CTX, back)

    dq, dk2, dv2 = pl.pallas_call(
        late_kernel,
        grid=(KV_HEADS // 2,),
        in_specs=[
            heads(ROWS, 2),
            heads(ROWS, 2),
            tile(rows),
            tile(rows),
            pl.BlockSpec((1, 1, GROUP * ROWS), lambda k: (2, 0, 0)),
            pl.BlockSpec(memory_space=pl.ANY),
        ],
        out_specs=[heads(ROWS, 2), tile(rows), tile(rows)],
        out_shape=[
            jax.ShapeDtypeStruct((rows, QUERY_HEADS * HEAD), bf16),
            jax.ShapeDtypeStruct((rows, KEYF), f32),
            jax.ShapeDtypeStruct((rows, KEYF), f32),
        ],
        input_output_aliases={5: 0},
        scratch_shapes=scratch(1),
        compiler_params=room(16),
        name="band_late",
    )(q, g, keys, v, lowest, dq)

    lin, own, send = pl.pallas_call(
        tail_kernel,
        out_shape=[
            jax.ShapeDtypeStruct((rows, KEYF), bf16),
            jax.ShapeDtypeStruct((parts * parts, KEYF // 2 // parts, dim // parts), f32),
            jax.ShapeDtypeStruct((parts * parts, KEYF // 2 // parts, dim // parts), bf16),
        ],
        scratch_shapes=[pltpu.VMEM((parts, rows, dim // parts), bf16)],
        compiler_params=room(16),
        name="tail",
    )(dk1, dk2, incoming, cos_table, sin_table, tokens, order)
    beside = pl.pallas_call(
        input_kernel,
        out_shape=[jax.ShapeDtypeStruct((rows, dim), bf16), jax.ShapeDtypeStruct((rows, KEYF), bf16)],
        compiler_params=room(8),
        name="input_grad",
    )(lin, order, mine, other, dv1, dv2, incoming)

    weight_grad, (input_grad, value_grad) = scattered_gradient(own, send, beside, width, sub)
    return dq[None], value_grad[None], input_grad[None], weight_grad.T


def solution(mesh):
    fine = Mesh(mesh.devices.reshape(4, 4, 4, 4, 2), ("zl", "y", "zh", "x", "core"))
    rows = P(DP, CTX, None)
    square = P(DP, CTX)
    return jax.shard_map(
        per_device,
        mesh=fine,
        in_specs=(rows, rows, rows, square, rows, P(DP, None)),
        out_specs=(rows, rows, rows, square),
        check_vma=False,
    )
```

```python
import jax
import jax.numpy as jnp
from jax import lax
from jax.experimental import pallas as pl
from jax.experimental.pallas import tpu as pltpu
from jax.sharding import Mesh
from jax.sharding import PartitionSpec as P

QUERY_HEADS = 32
KV_HEADS = 4
HEAD = 64
WINDOW = 128
KEYF = 256
GROUP = QUERY_HEADS // KV_HEADS
ROWS = 64
rope_base = 150000.0
masked_score = -1e30
bf16 = jnp.bfloat16
f32 = jnp.float32

DP = ("zl", "y")
CTX = ("zh", "x", "core")
Z = ("zl", "zh")
YX = ("y", "x")


def nt(a, b):
    return lax.dot_general(a, b, (((1,), (1,)), ((), ())), preferred_element_type=f32)


def nn(a, b):
    return lax.dot_general(a, b, (((1,), (0,)), ((), ())), preferred_element_type=f32)


def tn(a, b):
    return lax.dot_general(a, b, (((0,), (0,)), ((), ())), preferred_element_type=f32)


def swap_halves(x):
    lane = lax.broadcasted_iota(jnp.int32, x.shape, 1)
    width = x.shape[1]
    return jnp.where(lane % HEAD < HEAD // 2, pltpu.roll(x, width - HEAD // 2, 1), pltpu.roll(x, HEAD // 2, 1))


def pack(tokens_ref, packed_ref):
    parts, _, wide = packed_ref.shape
    width = wide // parts
    for y in range(parts):
        for zl in range(parts):
            at = (zl * parts + y) * width
            packed_ref[y, :, zl * width : (zl + 1) * width] = tokens_ref[:, at : at + width]


def half_linear(packed_ref, half_ref):
    parts, rows, wide = packed_ref.shape
    total = jnp.zeros((rows, KEYF // 2), f32)
    for y in range(parts):
        total += nt(packed_ref[y], half_ref[y * parts : (y + 1) * parts].reshape(KEYF // 2, wide))
    return total


def first_kernel(packed_ref, mine_ref, linear_ref):
    linear_ref[...] = half_linear(packed_ref, mine_ref)


def table(ref):
    return jnp.concatenate([ref[...], ref[...]], axis=1)


def project_kernel(packed_ref, other_ref, linear_ref, order_ref, cos_ref, sin_ref, keys_ref, edge_ref):
    rows = packed_ref.shape[1]
    gathered = jnp.concatenate([linear_ref[...], half_linear(packed_ref, other_ref)], axis=1)
    top = gathered.astype(bf16)
    rest = gathered - top.astype(f32)
    middle = rest.astype(bf16)
    bottom = (rest - middle.astype(f32)).astype(bf16)
    order = order_ref[...]
    linear = nn(top, order) + (nn(middle, order) + nn(bottom, order))
    keys = (linear * table(cos_ref) + swap_halves(linear) * table(sin_ref)).astype(bf16)
    keys_ref[...] = keys
    edge_ref[...] = keys[rows - WINDOW :]


def band_pairs(q_ref, g_ref, low_ref, dq_ref, bias_ref, kk_ref, vv_ref, dka_ref, dva_ref, fill):
    blocks = q_ref.shape[0] // ROWS
    span = ROWS + WINDOW
    lanes = GROUP * ROWS

    @pl.when(pl.program_id(0) == 0)
    def _():
        key_at = lax.broadcasted_iota(jnp.int32, (span, lanes), 0)
        last = lax.broadcasted_iota(jnp.int32, (1, lanes), 1) % ROWS + WINDOW
        for b in range(blocks):
            bias_ref[b] = jnp.where((key_at >= low_ref[b]) & (key_at <= last), 0.0, masked_score)

    lane = lax.broadcasted_iota(jnp.int32, (ROWS, 2 * HEAD), 1)
    low = jnp.where(lane < HEAD, 1.0, 0.0).astype(bf16)
    high = jnp.where(lane < HEAD, 0.0, 1.0).astype(bf16)

    def stacked(ref, b, head):
        parts = []
        for p in range(GROUP // 2):
            at = (head * GROUP // 2 + p) * 2 * HEAD
            pair = ref[b * ROWS : (b + 1) * ROWS, at : at + 2 * HEAD]
            parts += [pair * low, pair * high]
        return jnp.concatenate(parts, axis=0)

    for head in range(2):
        fill(head)
        dka_ref[head] = jnp.zeros_like(dka_ref[head])
        dva_ref[head] = jnp.zeros_like(dva_ref[head])
        for b in range(blocks):
            band = slice(b * ROWS, b * ROWS + span)
            keys = kk_ref[band, :]
            values = vv_ref[band, :]
            qs = stacked(q_ref, b, head)
            gs = stacked(g_ref, b, head)
            scores = nt(keys, qs) + bias_ref[b]
            weights = jnp.exp(scores - jnp.max(scores, axis=0, keepdims=True))
            probs = weights * (1.0 / jnp.sum(weights, axis=0, keepdims=True))
            probs_low = probs.astype(bf16)
            prob_grad = nt(values, gs)
            delta = jnp.sum(probs_low.astype(f32) * prob_grad, axis=0, keepdims=True)
            score_low = (probs * (prob_grad - delta)).astype(bf16)
            dva_ref[head, band, :] += nn(probs_low, gs)
            dka_ref[head, band, :] += nn(score_low, qs)
            dq = tn(score_low, keys)
            for p in range(GROUP // 2):
                at = (head * GROUP // 2 + p) * 2 * HEAD
                top = dq[2 * p * ROWS : (2 * p + 1) * ROWS]
                bottom = dq[(2 * p + 1) * ROWS : (2 * p + 2) * ROWS]
                dq_ref[b * ROWS : (b + 1) * ROWS, at : at + 2 * HEAD] = jnp.where(
                    lane < HEAD, top, bottom
                ).astype(bf16)

    def joined(ref):
        first, second = ref[0], ref[1]
        at = lax.broadcasted_iota(jnp.int32, first.shape, 1)
        first = first + pltpu.roll(first, HEAD, 1)
        second = second + pltpu.roll(second, HEAD, 1)
        return jnp.where(at < HEAD, first, second)

    return joined(dka_ref) * 0.125, joined(dva_ref)


def doubled(tile, head, scale):
    wide = tile.astype(f32) * scale
    at = lax.broadcasted_iota(jnp.int32, wide.shape, 1)
    return jnp.where(at // HEAD == head, wide, pltpu.roll(wide, HEAD, 1)).astype(bf16)


def early_kernel(
    q_ref, g_ref, k_ref, v_ref, prior_k_ref, prior_v_ref, low_ref,
    dq_ref, dk_ref, dv_ref, out_edge_ref,
    bias_ref, kk_ref, vv_ref, dka_ref, dva_ref,
):
    def fill(head):
        kk_ref[:WINDOW, :] = doubled(prior_k_ref[...], head, 0.125)
        kk_ref[WINDOW:, :] = doubled(k_ref[...], head, 0.125)
        vv_ref[:WINDOW, :] = doubled(prior_v_ref[...], head, 1.0)
        vv_ref[WINDOW:, :] = doubled(v_ref[...], head, 1.0)

    dk, dv = band_pairs(q_ref, g_ref, low_ref, dq_ref, bias_ref, kk_ref, vv_ref, dka_ref, dva_ref, fill)
    out_edge_ref[0] = dk[:WINDOW].astype(bf16)
    out_edge_ref[1] = dv[:WINDOW].astype(bf16)
    dk_ref[...] = dk[WINDOW:]
    dv_ref[...] = dv[WINDOW:]


def late_kernel(
    q_ref, g_ref, k_ref, v_ref, low_ref, _,
    dq_ref, dk_ref, dv_ref,
    bias_ref, kk_ref, vv_ref, dka_ref, dva_ref,
):
    def fill(head):
        kk_ref[...] = doubled(k_ref[...], head, 0.125)
        vv_ref[...] = doubled(v_ref[...], head, 1.0)

    dk, dv = band_pairs(q_ref, g_ref, low_ref, dq_ref, bias_ref, kk_ref, vv_ref, dka_ref, dva_ref, fill)
    dk_ref[...] = dk
    dv_ref[...] = dv


def total(early_ref, late_ref, edge):
    sums = late_ref[...]
    start = sums.shape[0] - WINDOW
    sums = jnp.concatenate([sums[:WINDOW] + early_ref[...], sums[WINDOW:]], axis=0)
    return jnp.concatenate([sums[:start], sums[start:] + edge.astype(f32)], axis=0)


def tail_kernel(
    early_ref, late_ref, edge_ref, cos_ref, sin_ref, tokens_ref, order_ref,
    lin_ref, own_ref, send_ref, packed_ref,
):
    parts, rows, wide = packed_ref.shape
    dk = total(early_ref, late_ref, edge_ref[0])
    lin = (dk * table(cos_ref) - swap_halves(dk) * table(sin_ref)).astype(bf16)
    lin_ref[...] = lin
    ordered = nt(order_ref[...], lin).astype(bf16)
    half = KEYF // 2
    block = (parts, half // parts, wide)
    pack(tokens_ref, packed_ref)
    for y in range(parts):
        to = slice(y * parts, (y + 1) * parts)
        own_ref[to] = nn(ordered[:half], packed_ref[y]).reshape(block)
        send_ref[to] = nn(ordered[half:], packed_ref[y]).reshape(block).astype(bf16)


def input_kernel(lin_ref, order_ref, mine_ref, other_ref, early_ref, late_ref, edge_ref, ig_ref, vg_ref):
    vg_ref[...] = total(early_ref, late_ref, edge_ref[1]).astype(bf16)
    parts = 4
    wide = mine_ref.shape[2]
    width = wide // parts
    half = KEYF // 2
    ordered = nt(lin_ref[...], order_ref[...]).astype(bf16)
    for y in range(parts):
        at = slice(y * parts, (y + 1) * parts)
        part = nn(ordered[:, :half], mine_ref[at].reshape(half, wide))
        part = (part + nn(ordered[:, half:], other_ref[at].reshape(half, wide))).astype(bf16)
        for zl in range(parts):
            at = (zl * parts + y) * width
            ig_ref[:, at : at + width] = part[:, zl * width : (zl + 1) * width]


def room(mib):
    return pltpu.CompilerParams(vmem_limit_bytes=mib << 20)


def spread(x, axes):
    peers = lax.axis_size(axes)
    return lax.all_to_all(jnp.broadcast_to(x[None], (peers,) + x.shape), axes, 0, 0, tiled=True)


def exchanged(x, axis):
    return lax.ppermute(x, axis, [(0, 1), (1, 0)])


def gathered_weight(block):
    width, sub = block.shape
    zl, zh = lax.axis_size("zl"), lax.axis_size("zh")
    along_z = spread(block.T, Z).reshape(zl, zh, sub, width)
    return spread(along_z.transpose(1, 2, 0, 3).reshape(zh * sub, zl * width), YX)


def summed(x, axes):
    return jnp.sum(lax.all_to_all(x, axes, 0, 0, tiled=True).astype(f32), axis=0)


def scattered_gradient(own, send, beside, width, sub):
    zl, zh = lax.axis_size("zl"), lax.axis_size("zh")
    other, beside = lax.optimization_barrier((exchanged(send, "core"), beside))
    both = (own + other.astype(f32)).astype(bf16)
    over_yx = summed(both, YX).astype(bf16)
    over_yx = over_yx.reshape(zh, sub, zl, width).transpose(2, 0, 1, 3)
    return summed(over_yx.reshape(zl * zh, sub, width), Z), beside


def per_device(tokens_in, queries, values_in, key_weight, out_grad, doc_ids):
    rows = tokens_in.shape[1]
    dim = tokens_in.shape[2]
    width, sub = key_weight.shape
    tokens, q, g, v = tokens_in[0], queries[0], out_grad[0], values_in[0]
    q = pltpu.with_memory_space_constraint(q, pltpu.HBM)
    g = pltpu.with_memory_space_constraint(g, pltpu.HBM)
    blocks = rows // ROWS
    parts = lax.axis_size("y")
    peers = lax.axis_size(CTX)
    along = [(i, i + 1) for i in range(peers - 1)]
    back = [(i + 1, i) for i in range(peers - 1)]
    prior_v = lax.ppermute(v[rows - WINDOW :], CTX, along)

    mine = gathered_weight(key_weight)
    mine, position, core, docs = lax.optimization_barrier(
        (mine, lax.axis_index(CTX), lax.axis_index("core"), doc_ids[0])
    )
    first_row = position * rows

    lane = jnp.arange(2 * HEAD, dtype=jnp.int32)
    exponent = (lane % (HEAD // 2)).astype(f32) * (-2.0 / HEAD)
    inverse_freq = jnp.power(f32(rope_base), exponent)
    angles = (first_row + jnp.arange(rows, dtype=jnp.int32)).astype(f32)[:, None] * inverse_freq[None, :]
    cos_table = jnp.cos(angles)
    sin_table = jnp.sin(angles) * jnp.where(lane % HEAD < HEAD // 2, -1.0, 1.0)[None, :]

    padded_docs = jnp.concatenate([jnp.full((WINDOW,), -1, jnp.int32), docs])
    band_docs = lax.dynamic_slice_in_dim(padded_docs, first_row, rows + WINDOW)
    lowest = jnp.sum((band_docs[:, None] < band_docs[None, WINDOW:]).astype(jnp.int32), axis=0)
    block_row = jnp.arange(rows, dtype=jnp.int32)
    lowest = jnp.maximum(lowest - block_row // ROWS * ROWS, block_row % ROWS)
    lowest = jnp.tile(lowest.reshape(blocks, 1, ROWS), (1, 1, GROUP))

    dest = jnp.arange(KEYF, dtype=jnp.int32)
    rel, dest_x, dest_zh, dest_j = dest // 128, dest // 32 % 4, dest // 8 % 4, dest % 8
    source = dest_zh * 64 + dest_x * 16 + (rel ^ core) * 8 + dest_j
    order = (source[:, None] == jnp.arange(KEYF, dtype=jnp.int32)[None, :]).astype(bf16)

    other = exchanged(mine, "core")
    packed = pl.pallas_call(
        pack,
        out_shape=jax.ShapeDtypeStruct((parts, rows, dim // parts), bf16),
        compiler_params=room(8),
        name="pack",
    )(tokens)
    linear = pl.pallas_call(
        first_kernel,
        out_shape=jax.ShapeDtypeStruct((rows, KEYF // 2), f32),
        compiler_params=room(16),
        name="project_own",
    )(packed, mine)
    keys, edge = pl.pallas_call(
        project_kernel,
        out_shape=[jax.ShapeDtypeStruct((rows, KEYF), bf16), jax.ShapeDtypeStruct((WINDOW, KEYF), bf16)],
        compiler_params=room(16),
        name="project",
    )(packed, other, linear, order, cos_table, sin_table)

    prior_k = lax.ppermute(edge, CTX, along)

    span = ROWS + WINDOW
    pair = 2 * HEAD
    wide = 2 * GROUP * HEAD

    def tile(size):
        return pl.BlockSpec((size, pair), lambda k: (0, k))

    def heads(size, at):
        return pl.BlockSpec((size, wide), lambda k: (at, k))

    def scratch(count):
        band = (count - 1) * ROWS + span
        return [
            pltpu.VMEM((count, span, GROUP * ROWS), f32),
            pltpu.VMEM((band, pair), bf16),
            pltpu.VMEM((band, pair), bf16),
            pltpu.VMEM((2, band, pair), f32),
            pltpu.VMEM((2, band, pair), f32),
        ]

    dq, dk1, dv1, out_edge = pl.pallas_call(
        early_kernel,
        grid=(KV_HEADS // 2,),
        in_specs=[
            heads(WINDOW, 0),
            heads(WINDOW, 0),
            tile(WINDOW),
            tile(WINDOW),
            tile(WINDOW),
            tile(WINDOW),
            pl.BlockSpec((2, 1, GROUP * ROWS), lambda k: (0, 0, 0)),
        ],
        out_specs=[heads(WINDOW, 0), tile(WINDOW), tile(WINDOW), pl.BlockSpec((2, WINDOW, pair), lambda k: (0, 0, k))],
        out_shape=[
            jax.ShapeDtypeStruct((rows, QUERY_HEADS * HEAD), bf16),
            jax.ShapeDtypeStruct((WINDOW, KEYF), f32),
            jax.ShapeDtypeStruct((WINDOW, KEYF), f32),
            jax.ShapeDtypeStruct((2, WINDOW, KEYF), bf16),
        ],
        scratch_shapes=scratch(2),
        compiler_params=room(16),
        name="band_early",
    )(q, g, keys, v, prior_k, prior_v, lowest)

    incoming = lax.ppermute(out_edge, CTX, back)

    dq, dk2, dv2 = pl.pallas_call(
        late_kernel,
        grid=(KV_HEADS // 2,),
        in_specs=[
            heads(ROWS, 2),
            heads(ROWS, 2),
            tile(rows),
            tile(rows),
            pl.BlockSpec((1, 1, GROUP * ROWS), lambda k: (2, 0, 0)),
            pl.BlockSpec(memory_space=pl.ANY),
        ],
        out_specs=[heads(ROWS, 2), tile(rows), tile(rows)],
        out_shape=[
            jax.ShapeDtypeStruct((rows, QUERY_HEADS * HEAD), bf16),
            jax.ShapeDtypeStruct((rows, KEYF), f32),
            jax.ShapeDtypeStruct((rows, KEYF), f32),
        ],
        input_output_aliases={5: 0},
        scratch_shapes=scratch(1),
        compiler_params=room(16),
        name="band_late",
    )(q, g, keys, v, lowest, dq)

    lin, own, send = pl.pallas_call(
        tail_kernel,
        out_shape=[
            jax.ShapeDtypeStruct((rows, KEYF), bf16),
            jax.ShapeDtypeStruct((parts * parts, KEYF // 2 // parts, dim // parts), f32),
            jax.ShapeDtypeStruct((parts * parts, KEYF // 2 // parts, dim // parts), bf16),
        ],
        scratch_shapes=[pltpu.VMEM((parts, rows, dim // parts), bf16)],
        compiler_params=room(16),
        name="tail",
    )(dk1, dk2, incoming, cos_table, sin_table, tokens, order)
    beside = pl.pallas_call(
        input_kernel,
        out_shape=[jax.ShapeDtypeStruct((rows, dim), bf16), jax.ShapeDtypeStruct((rows, KEYF), bf16)],
        compiler_params=room(8),
        name="input_grad",
    )(lin, order, mine, other, dv1, dv2, incoming)

    weight_grad, (input_grad, value_grad) = scattered_gradient(own, send, beside, width, sub)
    return dq[None], value_grad[None], input_grad[None], weight_grad.T


def solution(mesh):
    fine = Mesh(mesh.devices.reshape(4, 4, 4, 4, 2), ("zl", "y", "zh", "x", "core"))
    rows = P(DP, CTX, None)
    square = P(DP, CTX)
    return jax.shard_map(
        per_device,
        mesh=fine,
        in_specs=(rows, rows, rows, square, rows, P(DP, None)),
        out_specs=(rows, rows, rows, square),
        check_vma=False,
    )
```
